128 devices in a mesh: sx: 16 (over x, y), sy: 8 (over z, core).
Axes of the slice: x: 4, y: 4, z: 4, core: 2. Of those that a mesh axis runs over, the one named last changes fastest.
Arguments:
- features: bfloat16 [512, 256, 256], P('sx', 'sy'), may hold values from -6 to 6
- coarse_features: bfloat16 [128, 256], P(('sx', 'sy')), may hold values from -6 to 6
- fine_index: int32 [32, 16, 128], P('sx', 'sy'), may hold values from 0 to 6399, as said below
- own_order: int32 [32, 16, 256], P('sx', 'sy'), may hold values from 0 to 255, each once within a row
Outputs:
- factor: float32 [32, 16, 512, 256], P('sx', 'sy')
The draws below stay inside these ranges and needn't reach their ends.
Inputs may be any that keep to these rules, and one draw needn't show every extreme that they name: `fine_index`: the 128 entries of one supernode are distinct and each names a cell of the 80 by 80 window centred on its own block, outside that block (row f // 80, column f % 80 of the window).
All inputs are finite; a program needn't handle non-finite values.
Results may differ from the reference program's by a relative error of at most 0.0003.
Values may be sent and summed in bfloat16 or wider, within the bound.
A program may use at most 320 MiB of HBM per device.

```python
import jax
import jax.numpy as jnp
import numpy as np
from jax import lax

D = 256
SB = 16
SN = 256
REACH = 2
BX = 2
BY = 2
NF = 128
NC = 128
NX = 512
NY = 256
SUPX = 32
SUPY = 16
N_SY = 8


def draw_fine_index(key, part):
    win_side = (2 * REACH + 1) * SB
    low_edge = REACH * SB
    high_edge = (REACH + 1) * SB
    candidates = np.array([row_at * win_side + col_at for row_at in range(win_side) for col_at in range(win_side) if not (low_edge <= row_at < high_edge and low_edge <= col_at < high_edge)], dtype=np.int32)
    subkeys = jax.random.split(key, SUPX * SUPY)
    picks = jax.vmap(lambda one_key: jax.random.permutation(one_key, candidates.shape[0]))(subkeys)[:, :NF]
    values = jnp.asarray(candidates)[picks]
    return values.reshape(SUPX, SUPY, NF).astype(jnp.int32)


def level_of(key, shape, cuts, least, largest):
    loudness = 1.0
    for position, blocks in cuts:
        steps = jax.random.uniform(jax.random.fold_in(jax.random.fold_in(key, 6), position), (blocks,), jnp.float32, least / len(cuts), largest / len(cuts))
        loudness = loudness * jnp.repeat(jnp.exp(steps), shape[position] // blocks).reshape((-1,) + (1,) * (len(shape) - 1 - position))
    return loudness


def gaussian(stream_key, shape, width, limit, cuts=(), kind=jnp.bfloat16):
    loudness = level_of(stream_key, shape, cuts, -0.22, 0.18) if cuts else 1.0
    values = jax.random.normal(stream_key, shape, jnp.float32) * width * loudness
    return jnp.minimum(jnp.maximum(values, -limit), limit).astype(kind)


def setup_inputs(seed: int = 0) -> dict:
    key_list = jax.random.split(jax.random.key(seed), 5)
    features = gaussian(key_list[0], (NX, NY, D), 1.0, 6.0, ((0, 16), (1, 8)))
    coarse_features = gaussian(key_list[1], (NC, D), 1.0, 6.0, ((0, 128),))
    fine_index = draw_fine_index(jax.random.fold_in(key_list[4], 71), 0)
    own_order = jax.vmap(lambda own: jax.random.permutation(own, SN))(jax.random.split(key_list[3], SUPX * SUPY)).reshape((SUPX, SUPY, SN)).astype(jnp.int32)
    return {"features": features, "coarse_features": coarse_features, "fine_index": fine_index, "own_order": own_order}


NUGGET_VALUE = 0.3

def factor_blocks(point_set, own_count):
    points = point_set.astype(jnp.float32)
    gram = jnp.einsum('smd,snd->smn', points, points, precision=lax.Precision.HIGHEST)
    squares = jnp.diagonal(gram, axis1=1, axis2=2)
    feat_width = point_set.shape[2]
    total = point_set.shape[1]
    theta = jnp.exp(-(squares[:, :, None] + squares[:, None, :] - 2.0 * gram) / feat_width)
    theta = theta + NUGGET_VALUE * jnp.eye(total, dtype=jnp.float32)
    lower = jnp.linalg.cholesky(theta)
    target = jnp.concatenate([jnp.zeros((total - own_count, own_count), jnp.float32), jnp.eye(own_count, dtype=jnp.float32)], axis=0)

    def solve_one(lower_one):
        return jax.scipy.linalg.solve_triangular(lower_one, target, lower=True, trans='T')
    return jax.vmap(solve_one)(lower)

def reference(features, coarse_features, fine_index, own_order):
    grid_x, grid_y, feat_width = features.shape
    super_x, super_y, fine_count = fine_index.shape
    own_count = own_order.shape[2]
    win_side = (2 * REACH + 1) * SB
    start_x = (jnp.arange(super_x, dtype=jnp.int32) * SB)[:, None, None]
    start_y = (jnp.arange(super_y, dtype=jnp.int32) * SB)[None, :, None]
    fine_gx = (start_x - REACH * SB + fine_index // win_side) % grid_x
    fine_gy = (start_y - REACH * SB + fine_index % win_side) % grid_y
    own_gx = start_x + own_order // SB
    own_gy = start_y + own_order % SB
    chosen = jnp.concatenate([fine_gx * grid_y + fine_gy, own_gx * grid_y + own_gy], axis=2).astype(jnp.int32)
    chosen = chosen.reshape(super_x * super_y, fine_count + own_count)
    flat_rows = features.reshape(grid_x * grid_y, feat_width)
    group_size = BX * BY * N_SY
    groups = chosen.reshape(-1, group_size, fine_count + own_count)

    def one_group(indices):
        gathered = jnp.take(flat_rows, indices, axis=0)
        coarse_rows = jnp.broadcast_to(coarse_features[None], (group_size,) + coarse_features.shape)
        point_set = jnp.concatenate([coarse_rows, gathered], axis=1)
        return factor_blocks(point_set, own_count)
    result = lax.map(one_group, groups)
    return result.reshape(super_x, super_y, result.shape[2], result.shape[3])
```

```python
import jax
import jax.numpy as jnp
from jax import lax
from jax.experimental import pallas as pl
from jax.experimental.pallas import tpu as pltpu
from jax.sharding import PartitionSpec as P

SB = 16
REACH = 2
NUGGET = 0.3
BS = 32
F32 = jnp.float32
BF16 = jnp.bfloat16
HI = lax.Precision.HIGHEST
NN = (((1,), (0,)), ((), ()))
NT = (((1,), (1,)), ((), ()))


def mm(a, b, dims=NN):
    return lax.dot_general(a, b, dims, precision=HI, preferred_element_type=F32)


def bmm(a, b, dims=NN):
    return lax.dot_general(a, b, dims, preferred_element_type=F32)


def lane_pick(x, lane):
    at = (lax.broadcasted_iota(jnp.int32, x.shape, 1) // BS) * BS + lane
    return jnp.take_along_axis(x, at, axis=1)


def base_block(z):
    vs = [z[8 * v : 8 * v + 8] for v in range(4)]
    li = lax.broadcasted_iota(jnp.int32, (8, 128), 1) % BS
    si = lax.broadcasted_iota(jnp.int32, (8, 128), 0)
    factor = []
    for g in range(4):
        cols = [[lane_pick(vs[v], 8 * g + q) for v in range(4)] for q in range(8)]
        here = li // 8 == g
        eye = (li % 8 == si).astype(F32)
        vs = [jnp.where(here, eye if v == g else 0.0, vs[v]) for v in range(4)]
        rows = jnp.zeros((8, 128), F32)
        for q in range(8):
            piv = jnp.broadcast_to(cols[q][g][q : q + 1], (8, 128))
            rinv = 1.0 / piv
            plain = jnp.broadcast_to(vs[g][q : q + 1], (8, 128))
            rows = jnp.where(si == q, plain * lax.rsqrt(piv), rows)
            row = plain * rinv
            later = {p: jnp.broadcast_to(cols[p][g][q : q + 1], (8, 128)) * rinv for p in range(q + 1, 8)}
            for v in range(4):
                m = cols[q][v]
                vs[v] = vs[v] - m * row
                for p in later:
                    cols[p][v] = cols[p][v] - m * later[p]
                if v == g:
                    vs[v] = jnp.where(si == q, row, vs[v])
                    for p in later:
                        cols[p][v] = jnp.where(si == q, later[p], cols[p][v])
        factor.append(jnp.where(li <= si + 8 * g, rows, 0.0))
    return jnp.concatenate(vs, 0), jnp.concatenate(factor, 0)


def spread(x, diag):
    return jnp.where(diag, jnp.concatenate([x] * 4, 0), 0.0)


def inner(zp):
    diag = lax.broadcasted_iota(jnp.int32, (128, 128), 0) // BS == lax.broadcasted_iota(jnp.int32, (128, 128), 1) // BS
    zp = [[z[BS * t : BS * t + BS] for t in range(4)] for z in zp]
    out = []
    for t in range(4):
        dinv, w = base_block(zp[t][t])
        src = [spread(zp[u][t], diag) if u != t else None for u in range(4)]
        out.append([mm(w, src[u]) for u in range(t)] + [w] + [jnp.zeros_like(w)] * (3 - t))
        dspread = spread(dinv, diag)
        for i in range(t + 1, 4):
            g = mm(zp[t][i], dspread)
            for u in range(4):
                zp[u][i] = -g if u == t else zp[u][i] - mm(g, src[u])
    return out


def unpack(out, s):
    return jnp.concatenate(
        [jnp.concatenate([out[t][u][:, BS * s : BS * s + BS] for u in range(4)], 1) for t in range(4)], 0
    )


def pack(blocks):
    return [jnp.concatenate([b[:, BS * u : BS * u + BS] for b in blocks], 1) for u in range(4)]


def squares(x):
    xf = x.astype(F32)
    x2 = xf * xf
    hi = x2.astype(BF16)
    lo = (x2 - hi.astype(F32)).astype(BF16)
    ones = jnp.ones((8, x.shape[1]), BF16)
    row = (bmm(ones, hi, NT) + bmm(ones, lo, NT))[:1]
    return jnp.sum(x2, axis=1, keepdims=True), row


def theta(a, b, sa, sb, same):
    t = jnp.exp((2.0 * bmm(a, b, NT) - (sa + sb)) * (1.0 / a.shape[1]))
    if same:
        i, j = lax.broadcasted_iota(jnp.int32, t.shape, 0), lax.broadcasted_iota(jnp.int32, t.shape, 1)
        t = jnp.where(i == j, 1.0 + NUGGET, t)
    return t


def kernel(feat_ref, coarse_ref, fine_at_ref, own_at_ref, out_ref, acc_ref, fo_ref, k_ref, kt_ref, a_ref, lof_ref, e_ref):
    side = feat_ref.shape[0]
    width = feat_ref.shape[2]
    nf = 128
    pc = coarse_ref[...]
    sc_col, sc_row = squares(pc)
    acc_ref[...] = jnp.zeros_like(acc_ref)
    step_rows = 16
    chunk = step_rows * side

    def pick(c, carry):
        rows = feat_ref[pl.ds(c * step_rows, step_rows)].reshape(chunk, width)
        lane = lax.broadcasted_iota(jnp.int32, (4 * nf, chunk), 1) + c * chunk
        hot = jnp.where(lane == fine_at_ref[...], 1.0, 0.0).astype(BF16)
        acc_ref[...] += bmm(hot, rows)
        return carry

    lax.fori_loop(0, side // step_rows, pick, 0)
    for s in range(4):
        bx, by = divmod(s, 2)
        own = feat_ref[32 + 16 * bx : 48 + 16 * bx, 32 + 16 * by : 48 + 16 * by].reshape(256, width)
        hot = jnp.where(
            lax.broadcasted_iota(jnp.int32, (256, 256), 1) == own_at_ref[256 * s : 256 * s + 256], 1.0, 0.0
        ).astype(BF16)
        fo_ref[s, nf:] = bmm(hot, own).astype(BF16)
        fo_ref[s, :nf] = acc_ref[nf * s : nf * s + nf].astype(BF16)
    acc = theta(pc, pc, sc_col, sc_row, True)
    wc = unpack(inner(pack([acc] * 4)), 0)
    wct = wc.T
    for s in range(4):
        p = fo_ref[s]
        col, row = squares(p)
        kc = mm(theta(p, pc, col, sc_row, False), wc, NT)
        k_ref[s] = kc
        kt_ref[s] = mm(wc, theta(pc, p, sc_col, row, False))
        a_ref[s] = theta(p, p, col, row, True) - mm(kc, kc, NT)
    out = inner(pack([a_ref[s, :nf, :nf] for s in range(4)]))
    for s in range(4):
        wf = unpack(out, s)
        lof = mm(a_ref[s, nf:, :nf], wf, NT)
        lof_ref[s] = lof
        a_ref[s, nf:, nf:] = a_ref[s, nf:, nf:] - mm(lof, lof, NT)
        qft = mm(wf.T, mm(wf, a_ref[s, :nf, nf:]))
        e_ref[s, 128:256] = -qft
        e_ref[s, :128] = mm(wct, mm(kt_ref[s, :, :nf], qft) - kt_ref[s, :, nf:])
    out = inner(pack([a_ref[s, 128:256, 128:256] for s in range(4)]))
    for s in range(4):
        w0 = unpack(out, s)
        l10 = mm(a_ref[s, 256:, 128:256], w0, NT)
        lof_ref[s, :128] = l10
        a_ref[s, 256:, 256:] = a_ref[s, 256:, 256:] - mm(l10, l10, NT)
        top = mm(e_ref[s, :, :128], w0, NT)
        w0t = w0.T
        out_ref[s, :256, :128] = top
        out_ref[s, 256:384, :128] = w0t
        out_ref[s, 384:, :128] = jnp.zeros((128, 128), F32)
        e_ref[s, :, 128:] = e_ref[s, :, 128:] - mm(top, l10, NT)
        a_ref[s, :128, :128] = mm(w0t, l10, NT)
    out = inner(pack([a_ref[s, 256:, 256:] for s in range(4)]))
    for s in range(4):
        w1 = unpack(out, s)
        out_ref[s, :256, 128:] = mm(e_ref[s, :, 128:], w1, NT)
        out_ref[s, 256:384, 128:] = -mm(a_ref[s, :128, :128], w1, NT)
        out_ref[s, 384:, 128:] = w1.T


def padded_2(block, sides, width):
    for axis, dim in sides:
        count = lax.axis_size(axis)
        forward = [(i, (i + 1) % count) for i in range(count)]
        backward = [(target, source) for source, target in forward]
        low = lax.ppermute(
            lax.slice_in_dim(block, block.shape[dim] - width, None, axis=dim), axis, forward
        )
        high = lax.ppermute(lax.slice_in_dim(block, 0, width, axis=dim), axis, backward)
        block = jnp.concatenate([low, block, high], axis=dim)
    return block


def body(features, coarse_features, fine_index, own_order):
    block_x, block_y, fine_count = fine_index.shape
    rim = REACH * SB
    coarse = lax.all_gather(coarse_features, ("sx", "sy"), axis=0, tiled=True)
    padded = padded_2(features, (("sx", 0), ("sy", 1)), rim)
    side = padded.shape[1]
    win = (2 * REACH + 1) * SB
    start_x = (jnp.arange(block_x, dtype=jnp.int32) * SB)[:, None, None]
    start_y = (jnp.arange(block_y, dtype=jnp.int32) * SB)[None, :, None]
    fine_at = (start_x + fine_index // win) * side + start_y + fine_index % win
    vmem = pl.BlockSpec(memory_space=pltpu.VMEM)
    out = pl.pallas_call(
        kernel,
        out_shape=jax.ShapeDtypeStruct((4, 512, 256), F32),
        in_specs=[vmem] * 4,
        out_specs=vmem,
        scratch_shapes=[
            pltpu.VMEM((512, 256), F32),
            pltpu.VMEM((4, 384, 256), BF16),
            pltpu.VMEM((4, 384, 128), F32),
            pltpu.VMEM((4, 128, 384), F32),
            pltpu.VMEM((4, 384, 384), F32),
            pltpu.VMEM((4, 256, 128), F32),
            pltpu.VMEM((4, 256, 256), F32),
        ],
        compiler_params=pltpu.CompilerParams(vmem_limit_bytes=40 * 2**20),
    )(padded, coarse, fine_at.reshape(-1, 1), own_order.reshape(-1, 1))
    return out.reshape(block_x, block_y, 512, 256)


def solution(mesh):
    in_specs = (
        P("sx", "sy", None),
        P(("sx", "sy"), None),
        P("sx", "sy", None),
        P("sx", "sy", None),
    )
    out_specs = P("sx", "sy", None, None)
    return jax.shard_map(body, mesh=mesh, in_specs=in_specs, out_specs=out_specs, check_vma=False)
```

```python
import jax
import jax.numpy as jnp
from jax import lax
from jax.experimental import pallas as pl
from jax.experimental.pallas import tpu as pltpu
from jax.sharding import PartitionSpec as P

SB = 16
REACH = 2
NUGGET = 0.3
BS = 32
F32 = jnp.float32
BF16 = jnp.bfloat16
HI = lax.Precision.HIGHEST
NN = (((1,), (0,)), ((), ()))
NT = (((1,), (1,)), ((), ()))
MESH = pl.DeviceIdType.MESH
CHUNKS = 4


def mm(a, b, dims=NN):
    return lax.dot_general(a, b, dims, precision=HI, preferred_element_type=F32)


def bmm(a, b, dims=NN):
    return lax.dot_general(a, b, dims, preferred_element_type=F32)


def lane_pick(x, lane):
    at = (lax.broadcasted_iota(jnp.int32, x.shape, 1) // BS) * BS + lane
    return jnp.take_along_axis(x, at, axis=1)


def base_block(z):
    vs = [z[8 * v : 8 * v + 8] for v in range(4)]
    li = lax.broadcasted_iota(jnp.int32, (8, 128), 1) % BS
    si = lax.broadcasted_iota(jnp.int32, (8, 128), 0)
    factor = []
    for g in range(4):
        cols = [[lane_pick(vs[v], 8 * g + q) for v in range(4)] for q in range(8)]
        here = li // 8 == g
        eye = (li % 8 == si).astype(F32)
        vs = [jnp.where(here, eye if v == g else 0.0, vs[v]) for v in range(4)]
        rows = jnp.zeros((8, 128), F32)
        for q in range(8):
            piv = jnp.broadcast_to(cols[q][g][q : q + 1], (8, 128))
            rinv = 1.0 / piv
            plain = jnp.broadcast_to(vs[g][q : q + 1], (8, 128))
            rows = jnp.where(si == q, plain * lax.rsqrt(piv), rows)
            row = plain * rinv
            later = {p: jnp.broadcast_to(cols[p][g][q : q + 1], (8, 128)) * rinv for p in range(q + 1, 8)}
            for v in range(4):
                m = cols[q][v]
                vs[v] = vs[v] - m * row
                for p in later:
                    cols[p][v] = cols[p][v] - m * later[p]
                if v == g:
                    vs[v] = jnp.where(si == q, row, vs[v])
                    for p in later:
                        cols[p][v] = jnp.where(si == q, later[p], cols[p][v])
        factor.append(jnp.where(li <= si + 8 * g, rows, 0.0))
    return jnp.concatenate(vs, 0), jnp.concatenate(factor, 0)


def spread(x, diag):
    return jnp.where(diag, jnp.concatenate([x] * 4, 0), 0.0)


def inner(zp):
    diag = lax.broadcasted_iota(jnp.int32, (128, 128), 0) // BS == lax.broadcasted_iota(jnp.int32, (128, 128), 1) // BS
    zp = [[z[BS * t : BS * t + BS] for t in range(4)] for z in zp]
    out = []
    for t in range(4):
        dinv, w = base_block(zp[t][t])
        src = [spread(zp[u][t], diag) if u != t else None for u in range(4)]
        out.append([mm(w, src[u]) for u in range(t)] + [w] + [jnp.zeros_like(w)] * (3 - t))
        dspread = spread(dinv, diag)
        for i in range(t + 1, 4):
            g = mm(zp[t][i], dspread)
            for u in range(4):
                zp[u][i] = -g if u == t else zp[u][i] - mm(g, src[u])
    return out


def unpack(out, s):
    return jnp.concatenate(
        [jnp.concatenate([out[t][u][:, BS * s : BS * s + BS] for u in range(4)], 1) for t in range(4)], 0
    )


def pack(blocks):
    return [jnp.concatenate([b[:, BS * u : BS * u + BS] for b in blocks], 1) for u in range(4)]


def squares(x):
    xf = x.astype(F32)
    x2 = xf * xf
    hi = x2.astype(BF16)
    lo = (x2 - hi.astype(F32)).astype(BF16)
    ones = jnp.ones((8, x.shape[1]), BF16)
    row = (bmm(ones, hi, NT) + bmm(ones, lo, NT))[:1]
    return jnp.sum(x2, axis=1, keepdims=True), row


def theta(a, b, sa, sb, same):
    t = jnp.exp((2.0 * bmm(a, b, NT) - (sa + sb)) * (1.0 / a.shape[1]))
    if same:
        i, j = lax.broadcasted_iota(jnp.int32, t.shape, 0), lax.broadcasted_iota(jnp.int32, t.shape, 1)
        t = jnp.where(i == j, 1.0 + NUGGET, t)
    return t


def kernel(feat_ref, coarse_ref, fine_at_ref, own_at_ref, out_ref, acc_ref, fo_ref, k_ref, kt_ref, a_ref, lof_ref, e_ref):
    side = feat_ref.shape[0]
    width = feat_ref.shape[2]
    nf = 128
    pc = coarse_ref[...].reshape(128, width).astype(BF16)
    sc_col, sc_row = squares(pc)
    acc_ref[...] = jnp.zeros_like(acc_ref)
    step_rows = 16
    chunk = step_rows * side

    def pick(c, carry):
        rows = feat_ref[pl.ds(c * step_rows, step_rows)].reshape(chunk, width)
        lane = lax.broadcasted_iota(jnp.int32, (4 * nf, chunk), 1) + c * chunk
        hot = jnp.where(lane == fine_at_ref[...], 1.0, 0.0).astype(BF16)
        acc_ref[...] += bmm(hot, rows)
        return carry

    lax.fori_loop(0, side // step_rows, pick, 0)
    for s in range(4):
        bx, by = divmod(s, 2)
        own = feat_ref[32 + 16 * bx : 48 + 16 * bx, 32 + 16 * by : 48 + 16 * by].reshape(256, width)
        hot = jnp.where(
            lax.broadcasted_iota(jnp.int32, (256, 256), 1) == own_at_ref[256 * s : 256 * s + 256], 1.0, 0.0
        ).astype(BF16)
        fo_ref[s, nf:] = bmm(hot, own).astype(BF16)
        fo_ref[s, :nf] = acc_ref[nf * s : nf * s + nf].astype(BF16)
    acc = theta(pc, pc, sc_col, sc_row, True)
    wc = unpack(inner(pack([acc] * 4)), 0)
    wct = wc.T
    for s in range(4):
        p = fo_ref[s]
        col, row = squares(p)
        kc = mm(theta(p, pc, col, sc_row, False), wc, NT)
        k_ref[s] = kc
        kt_ref[s] = mm(wc, theta(pc, p, sc_col, row, False))
        a_ref[s] = theta(p, p, col, row, True) - mm(kc, kc, NT)
    out = inner(pack([a_ref[s, :nf, :nf] for s in range(4)]))
    for s in range(4):
        wf = unpack(out, s)
        lof = mm(a_ref[s, nf:, :nf], wf, NT)
        lof_ref[s] = lof
        a_ref[s, nf:, nf:] = a_ref[s, nf:, nf:] - mm(lof, lof, NT)
        qft = mm(wf.T, mm(wf, a_ref[s, :nf, nf:]))
        e_ref[s, 128:256] = -qft
        e_ref[s, :128] = mm(wct, mm(kt_ref[s, :, :nf], qft) - kt_ref[s, :, nf:])
    out = inner(pack([a_ref[s, 128:256, 128:256] for s in range(4)]))
    for s in range(4):
        w0 = unpack(out, s)
        l10 = mm(a_ref[s, 256:, 128:256], w0, NT)
        lof_ref[s, :128] = l10
        a_ref[s, 256:, 256:] = a_ref[s, 256:, 256:] - mm(l10, l10, NT)
        top = mm(e_ref[s, :, :128], w0, NT)
        w0t = w0.T
        out_ref[s, :256, :128] = top
        out_ref[s, 256:384, :128] = w0t
        out_ref[s, 384:, :128] = jnp.zeros((128, 128), F32)
        e_ref[s, :, 128:] = e_ref[s, :, 128:] - mm(top, l10, NT)
        a_ref[s, :128, :128] = mm(w0t, l10, NT)
    out = inner(pack([a_ref[s, 256:, 256:] for s in range(4)]))
    for s in range(4):
        w1 = unpack(out, s)
        out_ref[s, :256, 128:] = mm(e_ref[s, :, 128:], w1, NT)
        out_ref[s, 256:384, 128:] = -mm(a_ref[s, :128, :128], w1, NT)
        out_ref[s, 384:, 128:] = w1.T


def comm_kernel(feat_ref, coarse_ref, win_ref, all_ref, row_ref, a_send, a_recv, b_send, b_recv, x_send, x_recv, y_send, y_recv, f_send, f_recv, own_sem):
    nx, ny = lax.axis_size("sx"), lax.axis_size("sy")
    i, j = lax.axis_index("sx"), lax.axis_index("sy")
    rows, cols = feat_ref.shape[:2]
    part = rows // CHUNKS

    def at_x(step):
        return {"sx": lax.rem(i + step + nx, nx), "sy": j}

    def at_y(step):
        return {"sx": i, "sy": lax.rem(j + step + ny, ny)}

    def send(src, dst, s_sem, r_sem, device):
        copy = pltpu.make_async_remote_copy(
            src_ref=src, dst_ref=dst, send_sem=s_sem, recv_sem=r_sem, device_id=device, device_id_type=MESH
        )
        copy.start()
        return copy

    barrier = pltpu.get_barrier_semaphore()
    for k in range(1, ny):
        pl.semaphore_signal(barrier, inc=1, device_id=at_y(k), device_id_type=MESH)
    for k in range(1, nx):
        pl.semaphore_signal(barrier, inc=1, device_id=at_x(k), device_id_type=MESH)
    mine = pltpu.make_async_copy(feat_ref, win_ref.at[pl.ds(rows, rows), pl.ds(cols, cols)], own_sem.at[0])
    mine.start()
    row_ref[0] = coarse_ref[...].astype(F32)
    pl.semaphore_wait(barrier, nx + ny - 2)
    stage_a = [
        send(row_ref, all_ref.at[i, pl.ds(j, 1)], a_send.at[k], a_recv.at[k], at_y(k)) for k in range(1, ny)
    ]
    keep = pltpu.make_async_copy(row_ref, all_ref.at[i, pl.ds(j, 1)], own_sem.at[1])
    keep.start()
    along_x = []
    for c in range(CHUNKS):
        for d, step in enumerate((1, -1)):
            src = feat_ref.at[pl.ds(c * part, part)]
            dst = win_ref.at[pl.ds(2 * rows * d + c * part, part), pl.ds(cols, cols)]
            along_x.append(send(src, dst, x_send.at[d, c], x_recv.at[d, c], at_x(step)))
    along_y = []
    for d, step in enumerate((1, -1)):
        dst = win_ref.at[pl.ds(rows, rows), pl.ds(2 * cols * d, cols)]
        along_y.append(send(feat_ref, dst, y_send.at[d], y_recv.at[d], at_y(step)))
    keep.wait()
    for copy in stage_a:
        copy.wait()
    stage_b = [send(all_ref.at[i], all_ref.at[i], b_send.at[k], b_recv.at[k], at_x(k)) for k in range(1, nx)]
    onward = []
    for c in range(CHUNKS):
        for e in range(2):
            along_x[2 * c + e].wait()
            src = win_ref.at[pl.ds(2 * rows * e + c * part, part), pl.ds(cols, cols)]
            for d, step in enumerate((1, -1)):
                dst = win_ref.at[pl.ds(2 * rows * e + c * part, part), pl.ds(2 * cols * d, cols)]
                onward.append(send(src, dst, f_send.at[e, d, c], f_recv.at[e, d, c], at_y(step)))
    mine.wait()
    for copy in stage_b + along_y + onward:
        copy.wait()


def exchange(features, coarse_features):
    nx, ny = lax.axis_size("sx"), lax.axis_size("sy")
    rows, cols, width = features.shape
    dma = pltpu.SemaphoreType.DMA
    hbm = pl.BlockSpec(memory_space=pl.ANY)
    return pl.pallas_call(
        comm_kernel,
        out_shape=(
            jax.ShapeDtypeStruct((3 * rows, 3 * cols, width), features.dtype),
            jax.ShapeDtypeStruct((nx, ny, 1, width), F32),
        ),
        in_specs=[hbm, pl.BlockSpec(memory_space=pltpu.VMEM)],
        out_specs=(hbm, hbm),
        scratch_shapes=[
            pltpu.VMEM((1, 1, width), F32),
            dma((ny,)),
            dma((ny,)),
            dma((nx,)),
            dma((nx,)),
            dma((2, CHUNKS)),
            dma((2, CHUNKS)),
            dma((2,)),
            dma((2,)),
            dma((2, 2, CHUNKS)),
            dma((2, 2, CHUNKS)),
            dma((2,)),
        ],
        compiler_params=pltpu.CompilerParams(collective_id=0, has_side_effects=True),
    )(features, coarse_features)


def body(features, coarse_features, fine_index, own_order):
    block_x, block_y, fine_count = fine_index.shape
    padded, coarse = exchange(features, coarse_features)
    coarse = coarse.reshape(-1, 1, coarse.shape[3])
    side = padded.shape[1]
    win = (2 * REACH + 1) * SB
    start_x = (jnp.arange(block_x, dtype=jnp.int32) * SB)[:, None, None]
    start_y = (jnp.arange(block_y, dtype=jnp.int32) * SB)[None, :, None]
    fine_at = (start_x + fine_index // win) * side + start_y + fine_index % win
    vmem = pl.BlockSpec(memory_space=pltpu.VMEM)
    out = pl.pallas_call(
        kernel,
        out_shape=jax.ShapeDtypeStruct((4, 512, 256), F32),
        in_specs=[vmem] * 4,
        out_specs=vmem,
        scratch_shapes=[
            pltpu.VMEM((512, 256), F32),
            pltpu.VMEM((4, 384, 256), BF16),
            pltpu.VMEM((4, 384, 128), F32),
            pltpu.VMEM((4, 128, 384), F32),
            pltpu.VMEM((4, 384, 384), F32),
            pltpu.VMEM((4, 256, 128), F32),
            pltpu.VMEM((4, 256, 256), F32),
        ],
        compiler_params=pltpu.CompilerParams(vmem_limit_bytes=40 * 2**20),
    )(padded, coarse, fine_at.reshape(-1, 1), own_order.reshape(-1, 1))
    return out.reshape(block_x, block_y, 512, 256)


def solution(mesh):
    in_specs = (
        P("sx", "sy", None),
        P(("sx", "sy"), None),
        P("sx", "sy", None),
        P("sx", "sy", None),
    )
    out_specs = P("sx", "sy", None, None)
    return jax.shard_map(body, mesh=mesh, in_specs=in_specs, out_specs=out_specs, check_vma=False)
```

```python
import jax
import jax.numpy as jnp
from jax import lax
from jax.experimental import pallas as pl
from jax.experimental.pallas import tpu as pltpu
from jax.sharding import PartitionSpec as P

SB = 16
REACH = 2
NUGGET = 0.3
BS = 32
F32 = jnp.float32
BF16 = jnp.bfloat16
HI = lax.Precision.HIGHEST
NN = (((1,), (0,)), ((), ()))
NT = (((1,), (1,)), ((), ()))
MESH = pl.DeviceIdType.MESH


def mm(a, b, dims=NN):
    return lax.dot_general(a, b, dims, precision=HI, preferred_element_type=F32)


def bmm(a, b, dims=NN):
    return lax.dot_general(a, b, dims, preferred_element_type=F32)


def lane_pick(x, lane):
    at = (lax.broadcasted_iota(jnp.int32, x.shape, 1) // BS) * BS + lane
    return jnp.take_along_axis(x, at, axis=1)


def base_block(z):
    vs = [z[8 * v : 8 * v + 8] for v in range(4)]
    li = lax.broadcasted_iota(jnp.int32, (8, 128), 1) % BS
    si = lax.broadcasted_iota(jnp.int32, (8, 128), 0)
    factor = []
    for g in range(4):
        cols = [[lane_pick(vs[v], 8 * g + q) for v in range(4)] for q in range(8)]
        here = li // 8 == g
        eye = (li % 8 == si).astype(F32)
        vs = [jnp.where(here, eye if v == g else 0.0, vs[v]) for v in range(4)]
        rows = jnp.zeros((8, 128), F32)
        for q in range(8):
            piv = jnp.broadcast_to(cols[q][g][q : q + 1], (8, 128))
            rinv = 1.0 / piv
            plain = jnp.broadcast_to(vs[g][q : q + 1], (8, 128))
            rows = jnp.where(si == q, plain * lax.rsqrt(piv), rows)
            row = plain * rinv
            later = {p: jnp.broadcast_to(cols[p][g][q : q + 1], (8, 128)) * rinv for p in range(q + 1, 8)}
            for v in range(4):
                m = cols[q][v]
                vs[v] = vs[v] - m * row
                for p in later:
                    cols[p][v] = cols[p][v] - m * later[p]
                if v == g:
                    vs[v] = jnp.where(si == q, row, vs[v])
                    for p in later:
                        cols[p][v] = jnp.where(si == q, later[p], cols[p][v])
        factor.append(jnp.where(li <= si + 8 * g, rows, 0.0))
    return jnp.concatenate(vs, 0), jnp.concatenate(factor, 0)


def spread(x, diag):
    return jnp.where(diag, jnp.concatenate([x] * 4, 0), 0.0)


def inner(zp):
    diag = lax.broadcasted_iota(jnp.int32, (128, 128), 0) // BS == lax.broadcasted_iota(jnp.int32, (128, 128), 1) // BS
    zp = [[z[BS * t : BS * t + BS] for t in range(4)] for z in zp]
    out = []
    for t in range(4):
        dinv, w = base_block(zp[t][t])
        src = [spread(zp[u][t], diag) if u != t else None for u in range(4)]
        out.append([mm(w, src[u]) for u in range(t)] + [w] + [jnp.zeros_like(w)] * (3 - t))
        dspread = spread(dinv, diag)
        for i in range(t + 1, 4):
            g = mm(zp[t][i], dspread)
            for u in range(4):
                zp[u][i] = -g if u == t else zp[u][i] - mm(g, src[u])
    return out


def unpack(out, s):
    return jnp.concatenate(
        [jnp.concatenate([out[t][u][:, BS * s : BS * s + BS] for u in range(4)], 1) for t in range(4)], 0
    )


def pack(blocks):
    return [jnp.concatenate([b[:, BS * u : BS * u + BS] for b in blocks], 1) for u in range(4)]


def squares(x):
    xf = x.astype(F32)
    x2 = xf * xf
    hi = x2.astype(BF16)
    lo = (x2 - hi.astype(F32)).astype(BF16)
    ones = jnp.ones((8, x.shape[1]), BF16)
    row = (bmm(ones, hi, NT) + bmm(ones, lo, NT))[:1]
    return jnp.sum(x2, axis=1, keepdims=True), row


def theta(a, b, sa, sb, same):
    t = jnp.exp((2.0 * bmm(a, b, NT) - (sa + sb)) * (1.0 / a.shape[1]))
    if same:
        i, j = lax.broadcasted_iota(jnp.int32, t.shape, 0), lax.broadcasted_iota(jnp.int32, t.shape, 1)
        t = jnp.where(i == j, 1.0 + NUGGET, t)
    return t


def column(x):
    x = x.astype(F32)
    pad = jnp.zeros((8 - x.shape[0], x.shape[1]), F32)
    return jnp.concatenate([x, pad], 0).T


def kernel(feat_ref, coarse_ref, fine_ref, own_at_ref, out_ref, fo_ref, k_ref, kt_ref, a_ref, lof_ref, e_ref):
    width = feat_ref.shape[2]
    nf = 128
    pc = coarse_ref[...]
    sc_col, sc_row = squares(pc)
    own_at = column(own_at_ref[...])
    lane = lax.broadcasted_iota(jnp.int32, (256, 256), 1).astype(F32)
    for s in range(4):
        bx, by = divmod(s, 2)
        own = feat_ref[SB * bx : SB * bx + SB, SB * by : SB * by + SB].reshape(256, width)
        hot = jnp.where(lane == own_at[:, s : s + 1], 1.0, 0.0).astype(BF16)
        fo_ref[s, nf:] = bmm(hot, own).astype(BF16)
        fo_ref[s, :nf] = fine_ref[nf * s : nf * s + nf]
    acc = theta(pc, pc, sc_col, sc_row, True)
    wc = unpack(inner(pack([acc] * 4)), 0)
    wct = wc.T
    for s in range(4):
        p = fo_ref[s]
        col, row = squares(p)
        kc = mm(theta(p, pc, col, sc_row, False), wc, NT)
        k_ref[s] = kc
        kt_ref[s] = mm(wc, theta(pc, p, sc_col, row, False))
        a_ref[s] = theta(p, p, col, row, True) - mm(kc, kc, NT)
    out = inner(pack([a_ref[s, :nf, :nf] for s in range(4)]))
    for s in range(4):
        wf = unpack(out, s)
        lof = mm(a_ref[s, nf:, :nf], wf, NT)
        lof_ref[s] = lof
        a_ref[s, nf:, nf:] = a_ref[s, nf:, nf:] - mm(lof, lof, NT)
        qft = mm(wf.T, mm(wf, a_ref[s, :nf, nf:]))
        e_ref[s, 128:256] = -qft
        e_ref[s, :128] = mm(wct, mm(kt_ref[s, :, :nf], qft) - kt_ref[s, :, nf:])
    out = inner(pack([a_ref[s, 128:256, 128:256] for s in range(4)]))
    for s in range(4):
        w0 = unpack(out, s)
        l10 = mm(a_ref[s, 256:, 128:256], w0, NT)
        lof_ref[s, :128] = l10
        a_ref[s, 256:, 256:] = a_ref[s, 256:, 256:] - mm(l10, l10, NT)
        top = mm(e_ref[s, :, :128], w0, NT)
        w0t = w0.T
        out_ref[s, :256, :128] = top
        out_ref[s, 256:384, :128] = w0t
        out_ref[s, 384:, :128] = jnp.zeros((128, 128), F32)
        e_ref[s, :, 128:] = e_ref[s, :, 128:] - mm(top, l10, NT)
        a_ref[s, :128, :128] = mm(w0t, l10, NT)
    out = inner(pack([a_ref[s, 256:, 256:] for s in range(4)]))
    for s in range(4):
        w1 = unpack(out, s)
        out_ref[s, :256, 128:] = mm(e_ref[s, :, 128:], w1, NT)
        out_ref[s, 256:384, 128:] = -mm(a_ref[s, :128, :128], w1, NT)
        out_ref[s, 384:, 128:] = w1.T


OFFS = ((-1, -1), (-1, 0), (-1, 1), (0, -1), (0, 1), (1, -1), (1, 0), (1, 1))
CAPS = tuple(112 if 0 in o else 96 for o in OFFS)
STARTS = tuple(sum(CAPS[:n]) for n in range(9))


def comm_kernel(
    feat_ref, coarse_ref, fine_at_ref, fine_ref, coarse_out_ref, flag_ref,
    tile_ref, row_ref, all_ref, code_ref, codes_ref, out_ref, in_ref,
    a_send, a_recv, b_send, b_recv, c_send, c_recv, d_send, d_recv, tile_sem,
):
    nx, ny = lax.axis_size("sx"), lax.axis_size("sy")
    i, j = lax.axis_index("sx"), lax.axis_index("sy")
    rows, cols, width = feat_ref.shape
    cells = rows * cols
    asked = fine_at_ref.shape[0] * fine_at_ref.shape[1]

    def at(dx, dy):
        return {"sx": lax.rem(i + dx + nx, nx), "sy": lax.rem(j + dy + ny, ny)}

    def send(src, dst, s_sem, r_sem, device):
        copy = pltpu.make_async_remote_copy(
            src_ref=src, dst_ref=dst, send_sem=s_sem, recv_sem=r_sem, device_id=device, device_id_type=MESH
        )
        copy.start()
        return copy

    load = pltpu.make_async_copy(feat_ref, tile_ref, tile_sem)
    load.start()
    barrier = pltpu.get_barrier_semaphore()
    partners = [(dx, dy) for dx, dy in OFFS if dx and dy]
    partners += [(0, k) for k in range(1, ny)] + [(k, 0) for k in range(1, nx)]
    for dx, dy in partners:
        pl.semaphore_signal(barrier, inc=1, device_id=at(dx, dy), device_id_type=MESH)

    f = fine_at_ref[...]
    win_row = lax.shift_right_logical(f * 52429, 22)
    s_at = lax.broadcasted_iota(jnp.int32, f.shape, 0)
    r = win_row + SB * lax.shift_right_logical(s_at, 1)
    c = f - 80 * win_row + SB * lax.bitwise_and(s_at, 1)
    t9 = 3 * lax.shift_right_logical(r, 5) + lax.shift_right_logical(c, 5)
    code = cells * t9 + 32 * lax.bitwise_and(r, 31) + lax.bitwise_and(c, 31)
    code = code.astype(F32)
    code = jnp.concatenate([code[s : s + 1] for s in range(4)], 1)
    code_ref[0] = code
    before = jnp.where(
        lax.broadcasted_iota(jnp.int32, (asked, asked), 0) < lax.broadcasted_iota(jnp.int32, (asked, asked), 1), 1.0, 0.0
    ).astype(BF16)
    slot_at = lax.broadcasted_iota(jnp.int32, (8, asked), 0)

    def by_slot(values):
        out = jnp.zeros((8, asked), F32)
        for n, value in enumerate(values):
            out = jnp.where(slot_at == n, float(value), out)
        return out

    def ranks(offset):
        ok = jnp.logical_and(offset >= 0.0, offset < cells)
        return ok, bmm(jnp.where(ok, 1.0, 0.0).astype(BF16), before)

    offset = jnp.broadcast_to(code, (8, asked)) - by_slot([cells * (3 * (dx + 1) + dy + 1) for dx, dy in OFFS])
    ok, rank = ranks(offset)
    late = jnp.where(jnp.logical_and(ok, rank >= by_slot(CAPS)), 1.0, 0.0)
    late = jnp.sum(jnp.sum(late, axis=1, keepdims=True), axis=0, keepdims=True)
    slot = jnp.sum(jnp.where(ok, rank + by_slot(STARTS[:8]), 0.0), axis=0, keepdims=True)
    local = code - 4.0 * cells
    inside = jnp.logical_and(local >= 0.0, local < cells)
    where_at = column(jnp.concatenate([jnp.where(inside, -1.0, slot), jnp.where(inside, local, -1.0)], 0))
    row_ref[0, :, :width] = coarse_ref[...].astype(F32)
    row_ref[0, :, width:] = jnp.broadcast_to(late, (1, 128))
    pl.semaphore_wait(barrier, len(partners))

    asks = [
        send(code_ref, codes_ref.at[pl.ds(7 - n, 1)], c_send.at[n], c_recv.at[7 - n], at(*OFFS[n])) for n in range(8)
    ]
    stage_a = [
        send(row_ref, all_ref.at[i, pl.ds(j, 1)], a_send.at[k], a_recv.at[k], at(0, k)) for k in range(1, ny)
    ]
    all_ref[i, pl.ds(j, 1)] = row_ref[...]
    load.wait()
    tile = tile_ref[...].reshape(cells, width)
    lane = lax.broadcasted_iota(jnp.int32, (asked, cells), 1).astype(F32)
    fine = bmm(jnp.where(lane == where_at[:, 1:2], 1.0, 0.0).astype(BF16), tile)
    for ask in asks:
        ask.wait()
    codes = jnp.concatenate([codes_ref[n] for n in range(8)], 0)
    offset = codes - by_slot([cells * (3 * (1 - dx) + 1 - dy) for dx, dy in OFFS])
    ok, rank = ranks(offset)
    rank = jnp.where(ok, rank, -1.0)
    for copy in stage_a:
        copy.wait()
    stage_b = [send(all_ref.at[i], all_ref.at[i], b_send.at[k], b_recv.at[k], at(k, 0)) for k in range(1, nx)]
    moves = []
    for n in (0, 2, 5, 7, 1, 6, 3, 4):
        cap = CAPS[n]
        slots = lax.broadcasted_iota(jnp.int32, (cap, asked), 0).astype(F32)
        cell = jnp.sum(jnp.where(slots == rank[n : n + 1], offset[n : n + 1], 0.0), axis=1, keepdims=True)
        hot = jnp.where(lane[:cap] == cell, 1.0, 0.0).astype(BF16)
        out_ref[STARTS[n] : STARTS[n + 1]] = bmm(hot, tile).astype(BF16)
        moves.append(
            send(
                out_ref.at[pl.ds(STARTS[n], cap)],
                in_ref.at[pl.ds(STARTS[7 - n], cap)],
                d_send.at[n],
                d_recv.at[7 - n],
                at(*OFFS[n]),
            )
        )
    for copy in stage_b:
        copy.wait()
    full = all_ref[...].reshape(nx * ny, width + 128)
    coarse_out_ref[...] = full[:, :width].astype(BF16)
    flag_ref[...] = jnp.sum(full[:, width:], axis=0, keepdims=True)
    for copy in moves:
        copy.wait()
    got = in_ref[...]
    lane = lax.broadcasted_iota(jnp.int32, (asked, got.shape[0]), 1).astype(F32)
    fine = fine + bmm(jnp.where(lane == where_at[:, :1], 1.0, 0.0).astype(BF16), got)
    fine_ref[...] = fine.astype(BF16)


def exchange(features, coarse_features, fine_at):
    nx, ny = lax.axis_size("sx"), lax.axis_size("sy")
    rows, cols, width = features.shape
    asked = fine_at.shape[0] * fine_at.shape[1]
    dma = pltpu.SemaphoreType.DMA
    hbm = pl.BlockSpec(memory_space=pl.ANY)
    vmem = pl.BlockSpec(memory_space=pltpu.VMEM)
    return pl.pallas_call(
        comm_kernel,
        out_shape=(
            jax.ShapeDtypeStruct((asked, width), BF16),
            jax.ShapeDtypeStruct((nx * ny, width), BF16),
            jax.ShapeDtypeStruct((1, 128), F32),
        ),
        in_specs=[hbm, vmem, vmem],
        out_specs=(vmem, vmem, vmem),
        scratch_shapes=[
            pltpu.VMEM((rows, cols, width), BF16),
            pltpu.VMEM((1, 1, width + 128), F32),
            pltpu.VMEM((nx, ny, 1, width + 128), F32),
            pltpu.VMEM((1, 1, asked), F32),
            pltpu.VMEM((8, 1, asked), F32),
            pltpu.VMEM((STARTS[8], width), BF16),
            pltpu.VMEM((STARTS[8], width), BF16),
            dma((ny,)),
            dma((ny,)),
            dma((nx,)),
            dma((nx,)),
            dma((8,)),
            dma((8,)),
            dma((8,)),
            dma((8,)),
            dma,
        ],
        compiler_params=pltpu.CompilerParams(
            collective_id=0, has_side_effects=True, vmem_limit_bytes=32 * 2**20
        ),
    )(features, coarse_features, fine_at)


def padded_2(block, sides, width):
    for axis, dim in sides:
        count = lax.axis_size(axis)
        forward = [(i, (i + 1) % count) for i in range(count)]
        backward = [(target, source) for source, target in forward]
        low = lax.ppermute(
            lax.slice_in_dim(block, block.shape[dim] - width, None, axis=dim), axis, forward
        )
        high = lax.ppermute(lax.slice_in_dim(block, 0, width, axis=dim), axis, backward)
        block = jnp.concatenate([low, block, high], axis=dim)
    return block


def whole_tiles(features, fine_index):
    padded = padded_2(features, (("sx", 0), ("sy", 1)), REACH * SB)
    block_x, block_y = fine_index.shape[:2]
    win = (2 * REACH + 1) * SB
    start_x = (jnp.arange(block_x, dtype=jnp.int32) * SB)[:, None, None]
    start_y = (jnp.arange(block_y, dtype=jnp.int32) * SB)[None, :, None]
    at = (start_x + fine_index // win) * padded.shape[1] + start_y + fine_index % win
    return jnp.take(padded.reshape(-1, padded.shape[2]), at.reshape(-1), axis=0)


def body(features, coarse_features, fine_index, own_order):
    block_x, block_y, fine_count = fine_index.shape
    blocks = block_x * block_y
    fine, coarse, flag = exchange(features, coarse_features, fine_index.reshape(blocks, fine_count))
    fine = lax.cond(flag[0, 0] > 0.0, lambda f: whole_tiles(features, fine_index), lambda f: f, fine)
    vmem = pl.BlockSpec(memory_space=pltpu.VMEM)
    out = pl.pallas_call(
        kernel,
        out_shape=jax.ShapeDtypeStruct((4, 512, 256), F32),
        in_specs=[vmem] * 4,
        out_specs=vmem,
        scratch_shapes=[
            pltpu.VMEM((4, 384, 256), BF16),
            pltpu.VMEM((4, 384, 128), F32),
            pltpu.VMEM((4, 128, 384), F32),
            pltpu.VMEM((4, 384, 384), F32),
            pltpu.VMEM((4, 256, 128), F32),
            pltpu.VMEM((4, 256, 256), F32),
        ],
        compiler_params=pltpu.CompilerParams(vmem_limit_bytes=40 * 2**20),
    )(features, coarse, fine, own_order.reshape(blocks, -1))
    return out.reshape(block_x, block_y, 512, 256)


def solution(mesh):
    in_specs = (
        P("sx", "sy", None),
        P(("sx", "sy"), None),
        P("sx", "sy", None),
        P("sx", "sy", None),
    )
    out_specs = P("sx", "sy", None, None)
    return jax.shard_map(body, mesh=mesh, in_specs=in_specs, out_specs=out_specs, check_vma=False)
```

```python
import jax
import jax.numpy as jnp
from jax import lax
from jax.experimental import pallas as pl
from jax.experimental.pallas import tpu as pltpu
from jax.sharding import PartitionSpec as P

SB = 16
REACH = 2
NUGGET = 0.3
BS = 32
F32 = jnp.float32
BF16 = jnp.bfloat16
NN = (((1,), (0,)), ((), ()))
NT = (((1,), (1,)), ((), ()))
MESH = pl.DeviceIdType.MESH


def bmm(a, b, dims=NN):
    return lax.dot_general(a, b, dims, preferred_element_type=F32)


def split(x):
    hi = x.astype(BF16)
    rest = x - hi.astype(F32)
    mid = rest.astype(BF16)
    return hi, mid, (rest - mid.astype(F32)).astype(BF16)


def mm(a, b, dims=NN):
    (ca,), (cb,) = dims[0]
    a1, a2, a3 = split(a)
    b1, b2, b3 = split(b)
    return bmm(jnp.concatenate([a1, a1, a2, a2, a1, a3], ca), jnp.concatenate([b1, b2, b1, b2, b3, b1], cb), dims)


def lane_pick(x, lane):
    at = (lax.broadcasted_iota(jnp.int32, x.shape, 1) // BS) * BS + lane
    return jnp.take_along_axis(x, at, axis=1)


def sub_pick(x, q):
    return jnp.broadcast_to(x[q : q + 1], (8, 128))


def total(terms):
    while len(terms) > 1:
        terms = [sum(terms[k : k + 2][1:], terms[k]) for k in range(0, len(terms), 2)]
    return terms[0]


def base_block(z):
    vs = [z[8 * v : 8 * v + 8] for v in range(4)]
    li = lax.broadcasted_iota(jnp.int32, (8, 128), 1) % BS
    si = lax.broadcasted_iota(jnp.int32, (8, 128), 0)
    factor = []
    for h in range(2):
        group = (2 * h, 2 * h + 1)
        cols = [[lane_pick(vs[v], 16 * h + q) for v in range(4)] for q in range(16)]
        vs = [
            jnp.where(li // 16 == h, (li == si + 8 * v).astype(F32) if v in group else 0.0, vs[v]) for v in range(4)
        ]
        rows = [jnp.zeros((8, 128), F32)] * 2
        piv = sub_pick(cols[0][2 * h], 0)
        for q in range(16):
            g, sq = group[q // 8], q % 8
            rinv = 1.0 / piv
            plain = sub_pick(vs[g], sq)
            rows[q // 8] = jnp.where(si == sq, plain * lax.rsqrt(piv), rows[q // 8])
            later = {p: sub_pick(cols[p][g], sq) for p in range(q + 1, 16)}
            if q < 15:
                piv = sub_pick(cols[q + 1][group[(q + 1) // 8]], (q + 1) % 8) - later[q + 1] * later[q + 1] * rinv
            for v in group:
                m = cols[q][v]
                m = (jnp.where(si == sq, m - 1.0, m) if v == g else m) * rinv
                vs[v] = vs[v] - m * plain
                for p in later:
                    cols[p][v] = cols[p][v] - m * later[p]
        for v in range(4):
            if v not in group:
                vs[v] = vs[v] - total([cols[q][v] * sub_pick(vs[group[q // 8]], q % 8) for q in range(16)])
        factor += [jnp.where(li <= si + 8 * group[k], rows[k], 0.0) for k in range(2)]
    return jnp.concatenate(vs, 0), jnp.concatenate(factor, 0)


def spread(x, diag):
    return jnp.where(diag, jnp.concatenate([x] * 4, 0), 0.0)


def cut(x, i, u):
    return x[BS * i : BS * i + BS, BS * u : BS * u + BS]


def inner(blocks, hook):
    diag = lax.broadcasted_iota(jnp.int32, (128, 128), 0) // BS == lax.broadcasted_iota(jnp.int32, (128, 128), 1) // BS
    zp = [[None] * 4 for _ in range(4)]
    for u in range(4):
        for i in range(4):
            zp[u][i] = jnp.concatenate([cut(b, i, u) for b in blocks], 1)
    factor = [[] for _ in blocks]
    for t in range(4):
        hook(t)
        dinv, w = base_block(zp[t][t])
        src = [spread(zp[u][t], diag) if u != t else None for u in range(4)]
        if t < 3:
            g = mm(jnp.concatenate(zp[t][t + 1 :], 0), spread(dinv, diag))
            for u in sorted(range(4), key=lambda u: u != t + 1):
                change = g if u == t else mm(g, src[u])
                for i in range(t + 1, 4):
                    x = change[BS * (i - t - 1) : BS * (i - t)]
                    zp[u][i] = -x if u == t else zp[u][i] - x
        row = [mm(w, src[u]) for u in range(t)] + [w]
        for s in range(len(blocks)):
            parts = [x[:, BS * s : BS * s + BS] for x in row]
            parts += [jnp.zeros((BS, BS * (3 - t)), F32)] if t < 3 else []
            factor[s].append(jnp.concatenate(parts, 1))
    return [jnp.concatenate(f, 0) for f in factor]


def squares(x):
    xf = x.astype(F32)
    x2 = xf * xf
    hi = x2.astype(BF16)
    lo = (x2 - hi.astype(F32)).astype(BF16)
    ones = jnp.ones((8, x.shape[1]), BF16)
    row = (bmm(ones, hi, NT) + bmm(ones, lo, NT))[:1]
    return jnp.sum(x2, axis=1, keepdims=True), row


def theta(a, b, sa, sb, shift=None):
    t = jnp.exp((2.0 * bmm(a, b, NT) - (sa + sb)) * (1.0 / a.shape[1]))
    if shift is not None:
        i, j = lax.broadcasted_iota(jnp.int32, t.shape, 0), lax.broadcasted_iota(jnp.int32, t.shape, 1)
        t = jnp.where(i + shift == j, 1.0 + NUGGET, t)
    return t


def column(x):
    x = x.astype(F32)
    pad = jnp.zeros((8 - x.shape[0], x.shape[1]), F32)
    return jnp.concatenate([x, pad], 0).T


def kernel(feat_ref, coarse_ref, fine_ref, own_at_ref, out_ref, p_ref, k_ref, kt_ref, th_ref, e_ref):
    width = feat_ref.shape[2]
    n = 128
    four = range(4)
    pc = coarse_ref[...]
    sc_col, sc_row = squares(pc)
    own_at = column(own_at_ref[...])
    lane = lax.broadcasted_iota(jnp.int32, (256, 256), 1).astype(F32)

    def kernel_matrix(s):
        bx, by = divmod(s, 2)
        own = feat_ref[SB * bx : SB * bx + SB, SB * by : SB * by + SB].reshape(256, width)
        hot = jnp.where(lane == own_at[:, s : s + 1], 1.0, 0.0).astype(BF16)
        p_ref[s, n:] = bmm(hot, own).astype(BF16)
        p_ref[s, :n] = fine_ref[n * s : n * s + n]
        p = p_ref[s]
        col, row = squares(p)
        k_ref[s] = theta(p, pc, col, sc_row)
        kt_ref[s] = theta(pc, p, sc_col, row)
        th_ref[s, :, :n] = theta(p, p[:n], col, row[:, :n], 0)
        th_ref[s, n : 2 * n, n : 2 * n] = theta(p[n : 2 * n], p[n : 2 * n], col[n : 2 * n], row[:, n : 2 * n], 0)
        th_ref[s, 2 * n :, n:] = theta(p[2 * n :], p[n:], col[2 * n :], row[:, n:], n)

    wc = inner([theta(pc, pc, sc_col, sc_row, 0)] * 4, kernel_matrix)[0]

    kf = mm(jnp.concatenate([k_ref[s, :n] for s in four], 0), wc, NT)
    kf = [kf[n * s : n * s + n] for s in four]

    def leave_coarse(s):
        ko = mm(k_ref[s, n:], wc, NT)
        th_ref[s, n:, :n] = th_ref[s, n:, :n] - mm(ko, kf[s], NT)
        th_ref[s, n : 2 * n, n : 2 * n] = th_ref[s, n : 2 * n, n : 2 * n] - mm(ko[:n], ko[:n], NT)
        th_ref[s, 2 * n :, n:] = th_ref[s, 2 * n :, n:] - mm(ko[n:], ko, NT)

    wf = inner([th_ref[s, :n, :n] - mm(kf[s], kf[s], NT) for s in four], leave_coarse)

    lof = [mm(th_ref[s, n : 2 * n, :n], wf[s], NT) for s in four]
    cinv = mm(wc.T, wc)

    def leave_fine(s):
        low = mm(th_ref[s, 2 * n :, :n], wf[s], NT)
        both = jnp.concatenate([lof[s], low], 0)
        th_ref[s, 2 * n :, n:] = th_ref[s, 2 * n :, n:] - mm(low, both, NT)
        qt = mm(both, wf[s]).T
        ht = mm(cinv, kt_ref[s])
        e_ref[s, :n] = mm(ht[:, :n], qt) - ht[:, n:]
        e_ref[s, n : 2 * n] = -qt

    w0 = inner([th_ref[s, n : 2 * n, n : 2 * n] - mm(lof[s], lof[s], NT) for s in four], leave_fine)

    l10 = [mm(th_ref[s, 2 * n :, n : 2 * n], w0[s], NT) for s in four]

    def first_half(s):
        top = mm(e_ref[s, : 2 * n, :n], w0[s], NT)
        w0t = w0[s].T
        out_ref[s, : 2 * n, :n] = top
        out_ref[s, 2 * n : 3 * n, :n] = w0t
        out_ref[s, 3 * n :, :n] = jnp.zeros((n, n), F32)
        e_ref[s, : 2 * n, n:] = e_ref[s, : 2 * n, n:] - mm(top, l10[s], NT)
        e_ref[s, 2 * n :, n:] = -mm(w0t, l10[s], NT)

    w1 = inner([th_ref[s, 2 * n :, 2 * n :] - mm(l10[s], l10[s], NT) for s in four], first_half)
    for s in four:
        out_ref[s, : 3 * n, n:] = mm(e_ref[s, :, n:], w1[s], NT)
        out_ref[s, 3 * n :, n:] = w1[s].T


OFFS = ((-1, -1), (-1, 0), (-1, 1), (0, -1), (0, 1), (1, -1), (1, 0), (1, 1))
CAPS = tuple(112 if 0 in o else 96 for o in OFFS)
STARTS = tuple(sum(CAPS[:n]) for n in range(9))


def comm_kernel(
    feat_ref, coarse_ref, fine_at_ref, fine_ref, coarse_out_ref, flag_ref,
    tile_ref, row_ref, all_ref, code_ref, codes_ref, out_ref, in_ref,
    a_send, a_recv, b_send, b_recv, c_send, c_recv, d_send, d_recv, tile_sem,
):
    nx, ny = lax.axis_size("sx"), lax.axis_size("sy")
    i, j = lax.axis_index("sx"), lax.axis_index("sy")
    rows, cols, width = feat_ref.shape
    cells = rows * cols
    asked = fine_at_ref.shape[0] * fine_at_ref.shape[1]

    def at(dx, dy):
        return {"sx": lax.rem(i + dx + nx, nx), "sy": lax.rem(j + dy + ny, ny)}

    def send(src, dst, s_sem, r_sem, device):
        copy = pltpu.make_async_remote_copy(
            src_ref=src, dst_ref=dst, send_sem=s_sem, recv_sem=r_sem, device_id=device, device_id_type=MESH
        )
        copy.start()
        return copy

    load = pltpu.make_async_copy(feat_ref, tile_ref, tile_sem)
    load.start()
    barrier = pltpu.get_barrier_semaphore()
    partners = [(dx, dy) for dx, dy in OFFS if dx and dy]
    partners += [(0, k) for k in range(1, ny)] + [(k, 0) for k in range(1, nx)]
    for dx, dy in partners:
        pl.semaphore_signal(barrier, inc=1, device_id=at(dx, dy), device_id_type=MESH)

    f = fine_at_ref[...]
    win_row = lax.shift_right_logical(f * 52429, 22)
    s_at = lax.broadcasted_iota(jnp.int32, f.shape, 0)
    r = win_row + SB * lax.shift_right_logical(s_at, 1)
    c = f - 80 * win_row + SB * lax.bitwise_and(s_at, 1)
    t9 = 3 * lax.shift_right_logical(r, 5) + lax.shift_right_logical(c, 5)
    code = cells * t9 + 32 * lax.bitwise_and(r, 31) + lax.bitwise_and(c, 31)
    code = code.astype(F32)
    code = jnp.concatenate([code[s : s + 1] for s in range(4)], 1)
    code_ref[0] = code
    before = jnp.where(
        lax.broadcasted_iota(jnp.int32, (asked, asked), 0) < lax.broadcasted_iota(jnp.int32, (asked, asked), 1), 1.0, 0.0
    ).astype(BF16)
    slot_at = lax.broadcasted_iota(jnp.int32, (8, asked), 0)

    def by_slot(values):
        out = jnp.zeros((8, asked), F32)
        for n, value in enumerate(values):
            out = jnp.where(slot_at == n, float(value), out)
        return out

    def ranks(offset):
        ok = jnp.logical_and(offset >= 0.0, offset < cells)
        return ok, bmm(jnp.where(ok, 1.0, 0.0).astype(BF16), before)

    offset = jnp.broadcast_to(code, (8, asked)) - by_slot([cells * (3 * (dx + 1) + dy + 1) for dx, dy in OFFS])
    ok, rank = ranks(offset)
    late = jnp.where(jnp.logical_and(ok, rank >= by_slot(CAPS)), 1.0, 0.0)
    late = jnp.sum(jnp.sum(late, axis=1, keepdims=True), axis=0, keepdims=True)
    slot = jnp.sum(jnp.where(ok, rank + by_slot(STARTS[:8]), 0.0), axis=0, keepdims=True)
    local = code - 4.0 * cells
    inside = jnp.logical_and(local >= 0.0, local < cells)
    where_at = column(jnp.concatenate([jnp.where(inside, -1.0, slot), jnp.where(inside, local, -1.0)], 0))
    row_ref[0, :, :width] = coarse_ref[...].astype(F32)
    row_ref[0, :, width:] = jnp.broadcast_to(late, (1, 128))
    pl.semaphore_wait(barrier, len(partners))

    asks = [
        send(code_ref, codes_ref.at[pl.ds(7 - n, 1)], c_send.at[n], c_recv.at[7 - n], at(*OFFS[n])) for n in range(8)
    ]
    stage_a = [
        send(row_ref, all_ref.at[i, pl.ds(j, 1)], a_send.at[k], a_recv.at[k], at(0, k)) for k in range(1, ny)
    ]
    all_ref[i, pl.ds(j, 1)] = row_ref[...]
    load.wait()
    tile = tile_ref[...].reshape(cells, width)
    lane = lax.broadcasted_iota(jnp.int32, (asked, cells), 1).astype(F32)
    fine = bmm(jnp.where(lane == where_at[:, 1:2], 1.0, 0.0).astype(BF16), tile)
    for ask in asks:
        ask.wait()
    codes = jnp.concatenate([codes_ref[n] for n in range(8)], 0)
    offset = codes - by_slot([cells * (3 * (1 - dx) + 1 - dy) for dx, dy in OFFS])
    ok, rank = ranks(offset)
    rank = jnp.where(ok, rank, -1.0)
    for copy in stage_a:
        copy.wait()
    stage_b = [send(all_ref.at[i], all_ref.at[i], b_send.at[k], b_recv.at[k], at(k, 0)) for k in range(1, nx)]
    moves = []
    for n in (0, 2, 5, 7, 1, 6, 3, 4):
        cap = CAPS[n]
        slots = lax.broadcasted_iota(jnp.int32, (cap, asked), 0).astype(F32)
        cell = jnp.sum(jnp.where(slots == rank[n : n + 1], offset[n : n + 1], 0.0), axis=1, keepdims=True)
        hot = jnp.where(lane[:cap] == cell, 1.0, 0.0).astype(BF16)
        out_ref[STARTS[n] : STARTS[n + 1]] = bmm(hot, tile).astype(BF16)
        moves.append(
            send(
                out_ref.at[pl.ds(STARTS[n], cap)],
                in_ref.at[pl.ds(STARTS[7 - n], cap)],
                d_send.at[n],
                d_recv.at[7 - n],
                at(*OFFS[n]),
            )
        )
    for copy in stage_b:
        copy.wait()
    full = all_ref[...].reshape(nx * ny, width + 128)
    coarse_out_ref[...] = full[:, :width].astype(BF16)
    flag_ref[...] = jnp.sum(full[:, width:], axis=0, keepdims=True)
    for copy in moves:
        copy.wait()
    got = in_ref[...]
    lane = lax.broadcasted_iota(jnp.int32, (asked, got.shape[0]), 1).astype(F32)
    fine = fine + bmm(jnp.where(lane == where_at[:, :1], 1.0, 0.0).astype(BF16), got)
    fine_ref[...] = fine.astype(BF16)


def exchange(features, coarse_features, fine_at):
    nx, ny = lax.axis_size("sx"), lax.axis_size("sy")
    rows, cols, width = features.shape
    asked = fine_at.shape[0] * fine_at.shape[1]
    dma = pltpu.SemaphoreType.DMA
    hbm = pl.BlockSpec(memory_space=pl.ANY)
    vmem = pl.BlockSpec(memory_space=pltpu.VMEM)
    return pl.pallas_call(
        comm_kernel,
        out_shape=(
            jax.ShapeDtypeStruct((asked, width), BF16),
            jax.ShapeDtypeStruct((nx * ny, width), BF16),
            jax.ShapeDtypeStruct((1, 128), F32),
        ),
        in_specs=[hbm, vmem, vmem],
        out_specs=(vmem, vmem, vmem),
        scratch_shapes=[
            pltpu.VMEM((rows, cols, width), BF16),
            pltpu.VMEM((1, 1, width + 128), F32),
            pltpu.VMEM((nx, ny, 1, width + 128), F32),
            pltpu.VMEM((1, 1, asked), F32),
            pltpu.VMEM((8, 1, asked), F32),
            pltpu.VMEM((STARTS[8], width), BF16),
            pltpu.VMEM((STARTS[8], width), BF16),
            dma((ny,)),
            dma((ny,)),
            dma((nx,)),
            dma((nx,)),
            dma((8,)),
            dma((8,)),
            dma((8,)),
            dma((8,)),
            dma,
        ],
        compiler_params=pltpu.CompilerParams(
            collective_id=0, has_side_effects=True, vmem_limit_bytes=32 * 2**20
        ),
    )(features, coarse_features, fine_at)


def padded_2(block, sides, width):
    for axis, dim in sides:
        count = lax.axis_size(axis)
        forward = [(i, (i + 1) % count) for i in range(count)]
        backward = [(target, source) for source, target in forward]
        low = lax.ppermute(
            lax.slice_in_dim(block, block.shape[dim] - width, None, axis=dim), axis, forward
        )
        high = lax.ppermute(lax.slice_in_dim(block, 0, width, axis=dim), axis, backward)
        block = jnp.concatenate([low, block, high], axis=dim)
    return block


def whole_tiles(features, fine_index):
    padded = padded_2(features, (("sx", 0), ("sy", 1)), REACH * SB)
    block_x, block_y = fine_index.shape[:2]
    win = (2 * REACH + 1) * SB
    start_x = (jnp.arange(block_x, dtype=jnp.int32) * SB)[:, None, None]
    start_y = (jnp.arange(block_y, dtype=jnp.int32) * SB)[None, :, None]
    at = (start_x + fine_index // win) * padded.shape[1] + start_y + fine_index % win
    return jnp.take(padded.reshape(-1, padded.shape[2]), at.reshape(-1), axis=0)


def body(features, coarse_features, fine_index, own_order):
    block_x, block_y, fine_count = fine_index.shape
    blocks = block_x * block_y
    fine, coarse, flag = exchange(features, coarse_features, fine_index.reshape(blocks, fine_count))
    fine = lax.cond(flag[0, 0] > 0.0, lambda f: whole_tiles(features, fine_index), lambda f: f, fine)
    vmem = pl.BlockSpec(memory_space=pltpu.VMEM)
    out = pl.pallas_call(
        kernel,
        out_shape=jax.ShapeDtypeStruct((4, 512, 256), F32),
        in_specs=[vmem] * 4,
        out_specs=vmem,
        scratch_shapes=[
            pltpu.VMEM((4, 384, 256), BF16),
            pltpu.VMEM((4, 384, 128), F32),
            pltpu.VMEM((4, 128, 384), F32),
            pltpu.VMEM((4, 384, 384), F32),
            pltpu.VMEM((4, 384, 256), F32),
        ],
        compiler_params=pltpu.CompilerParams(vmem_limit_bytes=40 * 2**20),
    )(features, coarse, fine, own_order.reshape(blocks, -1))
    return out.reshape(block_x, block_y, 512, 256)


def solution(mesh):
    in_specs = (
        P("sx", "sy", None),
        P(("sx", "sy"), None),
        P("sx", "sy", None),
        P("sx", "sy", None),
    )
    out_specs = P("sx", "sy", None, None)
    return jax.shard_map(body, mesh=mesh, in_specs=in_specs, out_specs=out_specs, check_vma=False)
```

```python
import jax
import jax.numpy as jnp
from jax import lax
from jax.experimental import pallas as pl
from jax.experimental.pallas import tpu as pltpu
from jax.sharding import PartitionSpec as P

SB = 16
REACH = 2
NUGGET = 0.3
BS = 32
F32 = jnp.float32
BF16 = jnp.bfloat16
NN = (((1,), (0,)), ((), ()))
NT = (((1,), (1,)), ((), ()))
MESH = pl.DeviceIdType.MESH


def bmm(a, b, dims=NN):
    return lax.dot_general(a, b, dims, preferred_element_type=F32)


def mm(a, b, dims=NN):
    (ca,), (cb,) = dims[0]
    a1, b1 = a.astype(BF16), b.astype(BF16)
    a2, b2 = (a - a1.astype(F32)).astype(BF16), (b - b1.astype(F32)).astype(BF16)
    return bmm(jnp.concatenate([a1, a1, a2], ca), jnp.concatenate([b1, b2, b1], cb), dims)


def lane_pick(x, lane):
    at = (lax.broadcasted_iota(jnp.int32, x.shape, 1) // BS) * BS + lane
    return jnp.take_along_axis(x, at, axis=1)


def sub_pick(x, q):
    return jnp.broadcast_to(x[q : q + 1], (8, 128))


def total(terms):
    while len(terms) > 1:
        terms = [sum(terms[k : k + 2][1:], terms[k]) for k in range(0, len(terms), 2)]
    return terms[0]


def base_block(z):
    vs = [z[8 * v : 8 * v + 8] for v in range(4)]
    li = lax.broadcasted_iota(jnp.int32, (8, 128), 1) % BS
    si = lax.broadcasted_iota(jnp.int32, (8, 128), 0)
    factor = []
    for h in range(2):
        group = (2 * h, 2 * h + 1)
        cols = [[lane_pick(vs[v], 16 * h + q) for v in range(4)] for q in range(16)]
        vs = [
            jnp.where(li // 16 == h, (li == si + 8 * v).astype(F32) if v in group else 0.0, vs[v]) for v in range(4)
        ]
        rows = [jnp.zeros((8, 128), F32)] * 2
        piv = sub_pick(cols[0][2 * h], 0)
        for q in range(16):
            g, sq = group[q // 8], q % 8
            rinv = 1.0 / piv
            plain = sub_pick(vs[g], sq)
            rows[q // 8] = jnp.where(si == sq, plain * lax.rsqrt(piv), rows[q // 8])
            later = {p: sub_pick(cols[p][g], sq) for p in range(q + 1, 16)}
            if q < 15:
                piv = sub_pick(cols[q + 1][group[(q + 1) // 8]], (q + 1) % 8) - later[q + 1] * later[q + 1] * rinv
            for v in group:
                m = cols[q][v]
                m = (jnp.where(si == sq, m - 1.0, m) if v == g else m) * rinv
                vs[v] = vs[v] - m * plain
                for p in later:
                    cols[p][v] = cols[p][v] - m * later[p]
        for v in range(4):
            if v not in group:
                vs[v] = vs[v] - total([cols[q][v] * sub_pick(vs[group[q // 8]], q % 8) for q in range(16)])
        factor += [jnp.where(li <= si + 8 * group[k], rows[k], 0.0) for k in range(2)]
    return jnp.concatenate(vs, 0), jnp.concatenate(factor, 0)


def spread(x, diag):
    return jnp.where(diag, jnp.concatenate([x] * 4, 0), 0.0)


def cut(x, i, u):
    return x[BS * i : BS * i + BS, BS * u : BS * u + BS]


def inner(blocks, hook):
    diag = lax.broadcasted_iota(jnp.int32, (128, 128), 0) // BS == lax.broadcasted_iota(jnp.int32, (128, 128), 1) // BS
    zp = [[None] * 4 for _ in range(4)]
    for u in range(4):
        for i in range(4):
            zp[u][i] = jnp.concatenate([cut(b, i, u) for b in blocks], 1)
    factor = [[] for _ in blocks]
    for t in range(4):
        hook(t)
        dinv, w = base_block(zp[t][t])
        src = [spread(zp[u][t], diag) if u != t else None for u in range(4)]
        if t < 3:
            g = mm(jnp.concatenate(zp[t][t + 1 :], 0), spread(dinv, diag))
            for u in sorted(range(4), key=lambda u: u != t + 1):
                change = g if u == t else mm(g, src[u])
                for i in range(t + 1, 4):
                    x = change[BS * (i - t - 1) : BS * (i - t)]
                    zp[u][i] = -x if u == t else zp[u][i] - x
        row = [mm(w, src[u]) for u in range(t)] + [w]
        for s in range(len(blocks)):
            parts = [x[:, BS * s : BS * s + BS] for x in row]
            parts += [jnp.zeros((BS, BS * (3 - t)), F32)] if t < 3 else []
            factor[s].append(jnp.concatenate(parts, 1))
    return [jnp.concatenate(f, 0) for f in factor]


def squares(x):
    xf = x.astype(F32)
    x2 = xf * xf
    hi = x2.astype(BF16)
    lo = (x2 - hi.astype(F32)).astype(BF16)
    ones = jnp.ones((8, x.shape[1]), BF16)
    row = (bmm(ones, hi, NT) + bmm(ones, lo, NT))[:1]
    return jnp.sum(x2, axis=1, keepdims=True), row


def theta(a, b, sa, sb, shift=None):
    t = jnp.exp((2.0 * bmm(a, b, NT) - (sa + sb)) * (1.0 / a.shape[1]))
    if shift is not None:
        i, j = lax.broadcasted_iota(jnp.int32, t.shape, 0), lax.broadcasted_iota(jnp.int32, t.shape, 1)
        t = jnp.where(i + shift == j, 1.0 + NUGGET, t)
    return t


def column(x):
    x = x.astype(F32)
    pad = jnp.zeros((8 - x.shape[0], x.shape[1]), F32)
    return jnp.concatenate([x, pad], 0).T


def kernel(feat_ref, coarse_ref, fine_ref, own_at_ref, out_ref, p_ref, k_ref, kt_ref, th_ref, e_ref):
    width = feat_ref.shape[2]
    n = 128
    four = range(4)
    pc = coarse_ref[...]
    sc_col, sc_row = squares(pc)
    own_at = column(own_at_ref[...])
    lane = lax.broadcasted_iota(jnp.int32, (256, 256), 1).astype(F32)

    def kernel_matrix(s):
        bx, by = divmod(s, 2)
        own = feat_ref[SB * bx : SB * bx + SB, SB * by : SB * by + SB].reshape(256, width)
        hot = jnp.where(lane == own_at[:, s : s + 1], 1.0, 0.0).astype(BF16)
        p_ref[s, n:] = bmm(hot, own).astype(BF16)
        p_ref[s, :n] = fine_ref[n * s : n * s + n]
        p = p_ref[s]
        col, row = squares(p)
        k_ref[s] = theta(p, pc, col, sc_row)
        kt_ref[s] = theta(pc, p, sc_col, row)
        th_ref[s, :, :n] = theta(p, p[:n], col, row[:, :n], 0)
        th_ref[s, n : 2 * n, n : 2 * n] = theta(p[n : 2 * n], p[n : 2 * n], col[n : 2 * n], row[:, n : 2 * n], 0)
        th_ref[s, 2 * n :, n:] = theta(p[2 * n :], p[n:], col[2 * n :], row[:, n:], n)

    wc = inner([theta(pc, pc, sc_col, sc_row, 0)] * 4, kernel_matrix)[0]

    kf = mm(jnp.concatenate([k_ref[s, :n] for s in four], 0), wc, NT)
    kf = [kf[n * s : n * s + n] for s in four]

    def leave_coarse(s):
        ko = mm(k_ref[s, n:], wc, NT)
        th_ref[s, n:, :n] = th_ref[s, n:, :n] - mm(ko, kf[s], NT)
        th_ref[s, n : 2 * n, n : 2 * n] = th_ref[s, n : 2 * n, n : 2 * n] - mm(ko[:n], ko[:n], NT)
        th_ref[s, 2 * n :, n:] = th_ref[s, 2 * n :, n:] - mm(ko[n:], ko, NT)

    wf = inner([th_ref[s, :n, :n] - mm(kf[s], kf[s], NT) for s in four], leave_coarse)

    lof = [mm(th_ref[s, n : 2 * n, :n], wf[s], NT) for s in four]
    cinv = mm(wc.T, wc)

    def leave_fine(s):
        low = mm(th_ref[s, 2 * n :, :n], wf[s], NT)
        both = jnp.concatenate([lof[s], low], 0)
        th_ref[s, 2 * n :, n:] = th_ref[s, 2 * n :, n:] - mm(low, both, NT)
        qt = mm(both, wf[s]).T
        ht = mm(cinv, kt_ref[s])
        e_ref[s, :n] = mm(ht[:, :n], qt) - ht[:, n:]
        e_ref[s, n : 2 * n] = -qt

    w0 = inner([th_ref[s, n : 2 * n, n : 2 * n] - mm(lof[s], lof[s], NT) for s in four], leave_fine)

    l10 = [mm(th_ref[s, 2 * n :, n : 2 * n], w0[s], NT) for s in four]

    def first_half(s):
        top = mm(e_ref[s, : 2 * n, :n], w0[s], NT)
        w0t = w0[s].T
        out_ref[s, : 2 * n, :n] = top
        out_ref[s, 2 * n : 3 * n, :n] = w0t
        out_ref[s, 3 * n :, :n] = jnp.zeros((n, n), F32)
        e_ref[s, : 2 * n, n:] = e_ref[s, : 2 * n, n:] - mm(top, l10[s], NT)
        e_ref[s, 2 * n :, n:] = -mm(w0t, l10[s], NT)

    w1 = inner([th_ref[s, 2 * n :, 2 * n :] - mm(l10[s], l10[s], NT) for s in four], first_half)
    for s in four:
        out_ref[s, : 3 * n, n:] = mm(e_ref[s, :, n:], w1[s], NT)
        out_ref[s, 3 * n :, n:] = w1[s].T


OFFS = ((-1, -1), (-1, 1), (1, -1), (1, 1), (-1, 0), (0, -1), (0, 1), (1, 0))
BACK = (3, 2, 1, 0, 7, 6, 5, 4)
SIDE = 4
CAPS = tuple(112 if 0 in o else 96 for o in OFFS)
STARTS = tuple(sum(CAPS[:n]) for n in range(9))


def comm_kernel(
    feat_ref, coarse_ref, fine_at_ref, fine_ref, coarse_out_ref, flag_ref,
    tile_ref, row_ref, line_ref, all_ref, code_ref, codes_ref, out_ref, in_ref,
    a_send, a_recv, b_send, b_recv, c_send, c_recv, d_send, d_recv, tile_sem,
):
    nx, ny = lax.axis_size("sx"), lax.axis_size("sy")
    i, j = lax.axis_index("sx"), lax.axis_index("sy")
    rows, cols, width = feat_ref.shape
    cells = rows * cols
    asked = fine_at_ref.shape[0] * fine_at_ref.shape[1]

    def at(dx, dy):
        return {"sx": lax.rem(i + dx + nx, nx), "sy": lax.rem(j + dy + ny, ny)}

    def send(src, dst, s_sem, r_sem, device):
        copy = pltpu.make_async_remote_copy(
            src_ref=src, dst_ref=dst, send_sem=s_sem, recv_sem=r_sem, device_id=device, device_id_type=MESH
        )
        copy.start()
        return copy

    load = pltpu.make_async_copy(feat_ref, tile_ref, tile_sem)
    load.start()
    barrier = pltpu.get_barrier_semaphore()
    x, y = i // SIDE, lax.rem(i, SIDE)
    along_y = [lax.rem(y + k, SIDE) - y for k in range(1, SIDE)]
    along_x = [SIDE * k for k in range(1, nx // SIDE)]
    partners = [(dx, dy) for dx, dy in OFFS if dx]
    partners += [(0, k) for k in range(1, ny)] + [(k, 0) for k in along_y] + [(k, 0) for k in along_x]
    for dx, dy in partners:
        pl.semaphore_signal(barrier, inc=1, device_id=at(dx, dy), device_id_type=MESH)

    f = fine_at_ref[...]
    win_row = lax.shift_right_logical(f * 52429, 22)
    s_at = lax.broadcasted_iota(jnp.int32, f.shape, 0)
    r = win_row + SB * lax.shift_right_logical(s_at, 1)
    c = f - 80 * win_row + SB * lax.bitwise_and(s_at, 1)
    t9 = 3 * lax.shift_right_logical(r, 5) + lax.shift_right_logical(c, 5)
    code = cells * t9 + 32 * lax.bitwise_and(r, 31) + lax.bitwise_and(c, 31)
    code = code.astype(F32)
    code = jnp.concatenate([code[s : s + 1] for s in range(4)], 1)
    code_ref[0] = code
    before = jnp.where(
        lax.broadcasted_iota(jnp.int32, (asked, asked), 0) < lax.broadcasted_iota(jnp.int32, (asked, asked), 1), 1.0, 0.0
    ).astype(BF16)
    slot_at = lax.broadcasted_iota(jnp.int32, (8, asked), 0)

    def by_slot(values):
        out = jnp.zeros((8, asked), F32)
        for n, value in enumerate(values):
            out = jnp.where(slot_at == n, float(value), out)
        return out

    def ranks(offset):
        ok = jnp.logical_and(offset >= 0.0, offset < cells)
        return ok, bmm(jnp.where(ok, 1.0, 0.0).astype(BF16), before)

    offset = jnp.broadcast_to(code, (8, asked)) - by_slot([cells * (3 * (dx + 1) + dy + 1) for dx, dy in OFFS])
    ok, rank = ranks(offset)
    late = jnp.where(jnp.logical_and(ok, rank >= by_slot(CAPS)), 1.0, 0.0)
    late = jnp.sum(jnp.sum(late, axis=1, keepdims=True), axis=0, keepdims=True)
    slot = jnp.sum(jnp.where(ok, rank + by_slot(STARTS[:8]), 0.0), axis=0, keepdims=True)
    local = code - 4.0 * cells
    inside = jnp.logical_and(local >= 0.0, local < cells)
    where_at = column(jnp.concatenate([jnp.where(inside, -1.0, slot), jnp.where(inside, local, -1.0)], 0))
    row_ref[0, :, :width] = coarse_ref[...].astype(F32)
    row_ref[0, :, width:] = jnp.broadcast_to(late, (1, 128))
    pl.semaphore_wait(barrier, len(partners))

    asks = [
        send(code_ref, codes_ref.at[pl.ds(BACK[n], 1)], c_send.at[n], c_recv.at[BACK[n]], at(*OFFS[n])) for n in range(8)
    ]
    stage_a = [
        send(row_ref, line_ref.at[pl.ds(j, 1)], a_send.at[k], a_recv.at[k], at(0, k)) for k in range(1, ny)
    ]
    line_ref[pl.ds(j, 1)] = row_ref[...]
    load.wait()
    tile = tile_ref[...].reshape(cells, width)
    lane = lax.broadcasted_iota(jnp.int32, (asked, cells), 1).astype(F32)
    fine = bmm(jnp.where(lane == where_at[:, 1:2], 1.0, 0.0).astype(BF16), tile)
    for ask in asks:
        ask.wait()
    codes = jnp.concatenate([codes_ref[n] for n in range(8)], 0)
    offset = codes - by_slot([cells * (3 * (1 - dx) + 1 - dy) for dx, dy in OFFS])
    ok, rank = ranks(offset)
    rank = jnp.where(ok, rank, -1.0)
    for copy in stage_a:
        copy.wait()
    all_ref[i] = line_ref[...].reshape(ny, width + 128).astype(BF16)
    stage_b = [
        send(all_ref.at[i], all_ref.at[i], b_send.at[k], b_recv.at[k], at(step, 0)) for k, step in enumerate(along_y)
    ]
    moves = []
    for group in ((0, 1, 2, 3), (4, 5, 6, 7)):
        hot = []
        for n in group:
            slots = lax.broadcasted_iota(jnp.int32, (CAPS[n], asked), 0).astype(F32)
            cell = jnp.sum(jnp.where(slots == rank[n : n + 1], offset[n : n + 1], 0.0), axis=1, keepdims=True)
            hot.append(jnp.where(lane[: CAPS[n]] == cell, 1.0, 0.0).astype(BF16))
        low, high = STARTS[group[0]], STARTS[group[-1] + 1]
        out_ref[low:high] = bmm(jnp.concatenate(hot, 0), tile).astype(BF16)
        for n in group:
            src = out_ref.at[pl.ds(STARTS[n], CAPS[n])]
            dst = in_ref.at[pl.ds(STARTS[BACK[n]], CAPS[n])]
            moves.append(send(src, dst, d_send.at[n], d_recv.at[BACK[n]], at(*OFFS[n])))
    for copy in stage_b:
        copy.wait()
    lines = all_ref.at[pl.ds(SIDE * x, SIDE)]
    stage_c = [
        send(lines, lines, b_send.at[SIDE + k], b_recv.at[SIDE + k], at(step, 0)) for k, step in enumerate(along_x)
    ]
    lane = lax.broadcasted_iota(jnp.int32, (asked, STARTS[8]), 1).astype(F32)
    hot = jnp.where(lane == where_at[:, :1], 1.0, 0.0).astype(BF16)
    for copy in moves:
        copy.wait()
    fine_ref[...] = (fine + bmm(hot, in_ref[...])).astype(BF16)
    for copy in stage_c:
        copy.wait()
    full = all_ref[...].astype(F32).reshape(nx * ny, width + 128)
    coarse_out_ref[...] = full[:, :width].astype(BF16)
    flag_ref[...] = jnp.sum(full[:, width:], axis=0, keepdims=True)


def exchange(features, coarse_features, fine_at):
    nx, ny = lax.axis_size("sx"), lax.axis_size("sy")
    rows, cols, width = features.shape
    asked = fine_at.shape[0] * fine_at.shape[1]
    dma = pltpu.SemaphoreType.DMA
    hbm = pl.BlockSpec(memory_space=pl.ANY)
    vmem = pl.BlockSpec(memory_space=pltpu.VMEM)
    return pl.pallas_call(
        comm_kernel,
        out_shape=(
            jax.ShapeDtypeStruct((asked, width), BF16),
            jax.ShapeDtypeStruct((nx * ny, width), BF16),
            jax.ShapeDtypeStruct((1, 128), F32),
        ),
        in_specs=[hbm, vmem, vmem],
        out_specs=(vmem, vmem, vmem),
        scratch_shapes=[
            pltpu.VMEM((rows, cols, width), BF16),
            pltpu.VMEM((1, 1, width + 128), F32),
            pltpu.VMEM((ny, 1, width + 128), F32),
            pltpu.VMEM((nx, ny, width + 128), BF16),
            pltpu.VMEM((1, 1, asked), F32),
            pltpu.VMEM((8, 1, asked), F32),
            pltpu.VMEM((STARTS[8], width), BF16),
            pltpu.VMEM((STARTS[8], width), BF16),
            dma((ny,)),
            dma((ny,)),
            dma((2 * SIDE,)),
            dma((2 * SIDE,)),
            dma((8,)),
            dma((8,)),
            dma((8,)),
            dma((8,)),
            dma,
        ],
        compiler_params=pltpu.CompilerParams(
            collective_id=0, has_side_effects=True, vmem_limit_bytes=32 * 2**20
        ),
    )(features, coarse_features, fine_at)


def padded_2(block, sides, width):
    for axis, dim in sides:
        count = lax.axis_size(axis)
        forward = [(i, (i + 1) % count) for i in range(count)]
        backward = [(target, source) for source, target in forward]
        low = lax.ppermute(
            lax.slice_in_dim(block, block.shape[dim] - width, None, axis=dim), axis, forward
        )
        high = lax.ppermute(lax.slice_in_dim(block, 0, width, axis=dim), axis, backward)
        block = jnp.concatenate([low, block, high], axis=dim)
    return block


def whole_tiles(features, fine_index):
    padded = padded_2(features, (("sx", 0), ("sy", 1)), REACH * SB)
    block_x, block_y = fine_index.shape[:2]
    win = (2 * REACH + 1) * SB
    start_x = (jnp.arange(block_x, dtype=jnp.int32) * SB)[:, None, None]
    start_y = (jnp.arange(block_y, dtype=jnp.int32) * SB)[None, :, None]
    at = (start_x + fine_index // win) * padded.shape[1] + start_y + fine_index % win
    return jnp.take(padded.reshape(-1, padded.shape[2]), at.reshape(-1), axis=0)


def body(features, coarse_features, fine_index, own_order):
    block_x, block_y, fine_count = fine_index.shape
    blocks = block_x * block_y
    fine, coarse, flag = exchange(features, coarse_features, fine_index.reshape(blocks, fine_count))
    fine = lax.cond(flag[0, 0] > 0.0, lambda f: whole_tiles(features, fine_index), lambda f: f, fine)
    vmem = pl.BlockSpec(memory_space=pltpu.VMEM)
    out = pl.pallas_call(
        kernel,
        out_shape=jax.ShapeDtypeStruct((4, 512, 256), F32),
        in_specs=[vmem] * 4,
        out_specs=vmem,
        scratch_shapes=[
            pltpu.VMEM((4, 384, 256), BF16),
            pltpu.VMEM((4, 384, 128), F32),
            pltpu.VMEM((4, 128, 384), F32),
            pltpu.VMEM((4, 384, 384), F32),
            pltpu.VMEM((4, 384, 256), F32),
        ],
        compiler_params=pltpu.CompilerParams(vmem_limit_bytes=40 * 2**20),
    )(features, coarse, fine, own_order.reshape(blocks, -1))
    return out.reshape(block_x, block_y, 512, 256)


def solution(mesh):
    in_specs = (
        P("sx", "sy", None),
        P(("sx", "sy"), None),
        P("sx", "sy", None),
        P("sx", "sy", None),
    )
    out_specs = P("sx", "sy", None, None)
    return jax.shard_map(body, mesh=mesh, in_specs=in_specs, out_specs=out_specs, check_vma=False)
```

```python
import jax
import jax.numpy as jnp
from jax import lax
from jax.experimental import pallas as pl
from jax.experimental.pallas import tpu as pltpu
from jax.sharding import PartitionSpec as P

SB = 16
REACH = 2
NUGGET = 0.3
BS = 32
F32 = jnp.float32
BF16 = jnp.bfloat16
NN = (((1,), (0,)), ((), ()))
NT = (((1,), (1,)), ((), ()))
MESH = pl.DeviceIdType.MESH


def bmm(a, b, dims=NN):
    return lax.dot_general(a, b, dims, preferred_element_type=F32)


def mm(a, b, dims=NN):
    (ca,), (cb,) = dims[0]
    a1, b1 = a.astype(BF16), b.astype(BF16)
    a2, b2 = (a - a1.astype(F32)).astype(BF16), (b - b1.astype(F32)).astype(BF16)
    return bmm(jnp.concatenate([a1, a1, a2], ca), jnp.concatenate([b1, b2, b1], cb), dims)


def lane_pick(x, lane):
    at = (lax.broadcasted_iota(jnp.int32, x.shape, 1) // BS) * BS + lane
    return jnp.take_along_axis(x, at, axis=1)


def sub_pick(x, q):
    return jnp.broadcast_to(x[q : q + 1], (8, 128))


def total(terms):
    while len(terms) > 1:
        terms = [sum(terms[k : k + 2][1:], terms[k]) for k in range(0, len(terms), 2)]
    return terms[0]


def base_block(z):
    vs = [z[8 * v : 8 * v + 8] for v in range(4)]
    li = lax.broadcasted_iota(jnp.int32, (8, 128), 1) % BS
    si = lax.broadcasted_iota(jnp.int32, (8, 128), 0)
    factor = []
    for h in range(2):
        group = (2 * h, 2 * h + 1)
        cols = [[lane_pick(vs[v], 16 * h + q) for v in range(4)] for q in range(16)]
        vs = [
            jnp.where(li // 16 == h, (li == si + 8 * v).astype(F32) if v in group else 0.0, vs[v]) for v in range(4)
        ]
        rows = [jnp.zeros((8, 128), F32)] * 2
        piv = sub_pick(cols[0][2 * h], 0)
        for q in range(16):
            g, sq = group[q // 8], q % 8
            rinv = 1.0 / piv
            plain = sub_pick(vs[g], sq)
            rows[q // 8] = jnp.where(si == sq, plain * lax.rsqrt(piv), rows[q // 8])
            later = {p: sub_pick(cols[p][g], sq) for p in range(q + 1, 16)}
            if q < 15:
                piv = sub_pick(cols[q + 1][group[(q + 1) // 8]], (q + 1) % 8) - later[q + 1] * later[q + 1] * rinv
            for v in group:
                m = cols[q][v]
                m = (jnp.where(si == sq, m - 1.0, m) if v == g else m) * rinv
                vs[v] = vs[v] - m * plain
                for p in later:
                    cols[p][v] = cols[p][v] - m * later[p]
        for v in range(4):
            if v not in group:
                vs[v] = vs[v] - total([cols[q][v] * sub_pick(vs[group[q // 8]], q % 8) for q in range(16)])
        factor += [jnp.where(li <= si + 8 * group[k], rows[k], 0.0) for k in range(2)]
    return jnp.concatenate(vs, 0), jnp.concatenate(factor, 0)


def spread(x, diag):
    return jnp.where(diag, jnp.concatenate([x] * 4, 0), 0.0)


def cut(x, i, u):
    return x[BS * i : BS * i + BS, BS * u : BS * u + BS]


def inner(start, blocks, hook):
    diag = lax.broadcasted_iota(jnp.int32, (128, 128), 0) // BS == lax.broadcasted_iota(jnp.int32, (128, 128), 1) // BS
    zp = [[None] * 4 for _ in range(4)]
    zp[0][0] = jnp.concatenate(start, 1)
    factor = [[] for _ in start]
    for t in range(4):
        if t == 0:
            full = blocks()
            for u in range(4):
                for i in range(4):
                    if u or i:
                        zp[u][i] = jnp.concatenate([cut(b, i, u) for b in full], 1)
        hook(t)
        dinv, w = base_block(zp[t][t])
        src = [spread(zp[u][t], diag) if u != t else None for u in range(4)]
        if t < 3:
            g = mm(jnp.concatenate(zp[t][t + 1 :], 0), spread(dinv, diag))
            for u in sorted(range(4), key=lambda u: u != t + 1):
                change = g if u == t else mm(g, src[u])
                for i in range(t + 1, 4):
                    x = change[BS * (i - t - 1) : BS * (i - t)]
                    zp[u][i] = -x if u == t else zp[u][i] - x
        row = [mm(w, src[u]) for u in range(t)] + [w]
        for s in range(4):
            parts = [x[:, BS * s : BS * s + BS] for x in row]
            parts += [jnp.zeros((BS, BS * (3 - t)), F32)] if t < 3 else []
            factor[s].append(jnp.concatenate(parts, 1))
    return [jnp.concatenate(f, 0) for f in factor]


def squares(x):
    xf = x.astype(F32)
    x2 = xf * xf
    hi = x2.astype(BF16)
    lo = (x2 - hi.astype(F32)).astype(BF16)
    ones = jnp.ones((8, x.shape[1]), BF16)
    row = (bmm(ones, hi, NT) + bmm(ones, lo, NT))[:1]
    return jnp.sum(x2, axis=1, keepdims=True), row


def theta(a, b, sa, sb, shift=None):
    t = jnp.exp((2.0 * bmm(a, b, NT) - (sa + sb)) * (1.0 / a.shape[1]))
    if shift is not None:
        i, j = lax.broadcasted_iota(jnp.int32, t.shape, 0), lax.broadcasted_iota(jnp.int32, t.shape, 1)
        t = jnp.where(i + shift == j, 1.0 + NUGGET, t)
    return t


def column(x):
    x = x.astype(F32)
    pad = jnp.zeros((8 - x.shape[0], x.shape[1]), F32)
    return jnp.concatenate([x, pad], 0).T


def kernel(
    feat_hbm, coarse_ref, fine_ref, own_hbm, out_hbm,
    p_ref, k_ref, kt_ref, th_ref, e_ref, feat_ref, own_ref, lo_ref, hi_ref, in_sem, lo_sem, hi_sem,
):
    loads = [
        pltpu.make_async_copy(own_hbm, own_ref, in_sem.at[0]),
        pltpu.make_async_copy(feat_hbm, feat_ref, in_sem.at[1]),
    ]
    for load in loads:
        load.start()
    width = feat_ref.shape[2]
    n = 128
    four = range(4)
    pc = coarse_ref[...]
    sc_col, sc_row = squares(pc)
    acc = theta(pc, pc, sc_col, sc_row, 0)
    for load in loads:
        load.wait()
    own_at = column(jnp.concatenate([own_ref[0], own_ref[1]], 0))
    lane = lax.broadcasted_iota(jnp.int32, (256, 256), 1).astype(F32)

    def kernel_matrix(s):
        bx, by = divmod(s, 2)
        own = feat_ref[SB * bx : SB * bx + SB, SB * by : SB * by + SB].reshape(256, width)
        hot = jnp.where(lane == own_at[:, s : s + 1], 1.0, 0.0).astype(BF16)
        p_ref[s, n:] = bmm(hot, own).astype(BF16)
        p_ref[s, :n] = fine_ref[n * s : n * s + n]
        p = p_ref[s]
        col, row = squares(p)
        k_ref[s] = theta(p, pc, col, sc_row)
        kt_ref[s] = theta(pc, p, sc_col, row)
        th_ref[s, :, :n] = theta(p, p[:n], col, row[:, :n], 0)
        th_ref[s, n : 2 * n, n : 2 * n] = theta(p[n : 2 * n], p[n : 2 * n], col[n : 2 * n], row[:, n : 2 * n], 0)
        th_ref[s, 2 * n :, n:] = theta(p[2 * n :], p[n:], col[2 * n :], row[:, n:], n)

    wc = inner([cut(acc, 0, 0)] * 4, lambda: [acc] * 4, kernel_matrix)[0]

    def leading(rows, s, at):
        own = rows[BS * s : BS * s + BS]
        return th_ref[s, at : at + BS, at : at + BS] - mm(own, own, NT)

    kf = []

    def fine_block():
        x = mm(jnp.concatenate([k_ref[s, :n] for s in four], 0), wc, NT)
        kf.extend(x[n * s : n * s + n] for s in four)
        return [th_ref[s, :n, :n] - mm(kf[s], kf[s], NT) for s in four]

    def leave_coarse(s):
        ko = mm(k_ref[s, n:], wc, NT)
        th_ref[s, n:, :n] = th_ref[s, n:, :n] - mm(ko, kf[s], NT)
        th_ref[s, n : 2 * n, n : 2 * n] = th_ref[s, n : 2 * n, n : 2 * n] - mm(ko[:n], ko[:n], NT)
        th_ref[s, 2 * n :, n:] = th_ref[s, 2 * n :, n:] - mm(ko[n:], ko, NT)

    head = mm(jnp.concatenate([k_ref[s, :BS] for s in four], 0), wc, NT)
    wf = inner([leading(head, s, 0) for s in four], fine_block, leave_coarse)

    lof = []
    cinv = mm(wc.T, wc)

    def own_block():
        lof.extend(mm(th_ref[s, n : 2 * n, :n], wf[s], NT) for s in four)
        return [th_ref[s, n : 2 * n, n : 2 * n] - mm(lof[s], lof[s], NT) for s in four]

    def leave_fine(s):
        low = mm(th_ref[s, 2 * n :, :n], wf[s], NT)
        both = jnp.concatenate([lof[s], low], 0)
        th_ref[s, 2 * n :, n:] = th_ref[s, 2 * n :, n:] - mm(low, both, NT)
        qt = mm(both, wf[s]).T
        ht = mm(cinv, kt_ref[s])
        e_ref[s, :n] = mm(ht[:, :n], qt) - ht[:, n:]
        e_ref[s, n : 2 * n] = -qt

    head = jnp.concatenate([mm(th_ref[s, n : n + BS, :n], wf[s], NT) for s in four], 0)
    w0 = inner([leading(head, s, n) for s in four], own_block, leave_fine)

    l10 = []
    stores = []

    def last_block():
        l10.extend(mm(th_ref[s, 2 * n :, n : 2 * n], w0[s], NT) for s in four)
        return [th_ref[s, 2 * n :, 2 * n :] - mm(l10[s], l10[s], NT) for s in four]

    def first_half(s):
        top = mm(e_ref[s, : 2 * n, :n], w0[s], NT)
        w0t = w0[s].T
        lo_ref[s, : 2 * n] = top
        lo_ref[s, 2 * n : 3 * n] = w0t
        lo_ref[s, 3 * n :] = jnp.zeros((n, n), F32)
        stores.append(pltpu.make_async_copy(lo_ref.at[s], out_hbm.at[s, :, pl.ds(0, n)], lo_sem.at[s]))
        stores[-1].start()
        e_ref[s, : 2 * n, n:] = e_ref[s, : 2 * n, n:] - mm(top, l10[s], NT)
        e_ref[s, 2 * n :, n:] = -mm(w0t, l10[s], NT)

    head = jnp.concatenate([mm(th_ref[s, 2 * n : 2 * n + BS, n : 2 * n], w0[s], NT) for s in four], 0)
    w1 = inner([leading(head, s, 2 * n) for s in four], last_block, first_half)
    for s in four:
        hi_ref[s, : 3 * n] = mm(e_ref[s, :, n:], w1[s], NT)
        hi_ref[s, 3 * n :] = w1[s].T
        stores.append(pltpu.make_async_copy(hi_ref.at[s], out_hbm.at[s, :, pl.ds(n, n)], hi_sem.at[s]))
        stores[-1].start()
    for store in stores:
        store.wait()


OFFS = ((-1, -1), (-1, 1), (1, -1), (1, 1), (-1, 0), (0, -1), (0, 1), (1, 0))
BACK = (3, 2, 1, 0, 7, 6, 5, 4)
SIDE = 4
CAPS = tuple(112 if 0 in o else 96 for o in OFFS)
STARTS = tuple(sum(CAPS[:n]) for n in range(9))


def comm_kernel(
    feat_ref, coarse_hbm, fine_at_hbm, fine_ref, coarse_out_ref, flag_ref,
    tile_ref, row_ref, line_ref, all_ref, code_ref, codes_ref, out_ref, in_ref,
    a_send, a_recv, b_send, b_recv, c_send, c_recv, d_send, d_recv, tile_sem, coarse_ref, fine_at_ref, in_sem,
):
    nx, ny = lax.axis_size("sx"), lax.axis_size("sy")
    i, j = lax.axis_index("sx"), lax.axis_index("sy")
    rows, cols, width = feat_ref.shape
    cells = rows * cols
    asked = fine_at_ref.shape[0] * fine_at_ref.shape[1]

    def at(dx, dy):
        return {"sx": lax.rem(i + dx + nx, nx), "sy": lax.rem(j + dy + ny, ny)}

    def send(src, dst, s_sem, r_sem, device):
        copy = pltpu.make_async_remote_copy(
            src_ref=src, dst_ref=dst, send_sem=s_sem, recv_sem=r_sem, device_id=device, device_id_type=MESH
        )
        copy.start()
        return copy

    small = [
        pltpu.make_async_copy(fine_at_hbm, fine_at_ref, in_sem.at[0]),
        pltpu.make_async_copy(coarse_hbm, coarse_ref, in_sem.at[1]),
    ]
    for copy in small:
        copy.start()
    load = pltpu.make_async_copy(feat_ref, tile_ref, tile_sem)
    load.start()
    barrier = pltpu.get_barrier_semaphore()
    x, y = i // SIDE, lax.rem(i, SIDE)
    along_y = [lax.rem(y + k, SIDE) - y for k in range(1, SIDE)]
    along_x = [SIDE * k for k in range(1, nx // SIDE)]
    partners = [(dx, dy) for dx, dy in OFFS if dx]
    partners += [(0, k) for k in range(1, ny)] + [(k, 0) for k in along_y] + [(k, 0) for k in along_x]
    for dx, dy in partners:
        pl.semaphore_signal(barrier, inc=1, device_id=at(dx, dy), device_id_type=MESH)

    for copy in small:
        copy.wait()
    f = fine_at_ref[...]
    win_row = lax.shift_right_logical(f * 52429, 22)
    s_at = lax.broadcasted_iota(jnp.int32, f.shape, 0)
    r = win_row + SB * lax.shift_right_logical(s_at, 1)
    c = f - 80 * win_row + SB * lax.bitwise_and(s_at, 1)
    t9 = 3 * lax.shift_right_logical(r, 5) + lax.shift_right_logical(c, 5)
    code = cells * t9 + 32 * lax.bitwise_and(r, 31) + lax.bitwise_and(c, 31)
    code = code.astype(F32)
    code = jnp.concatenate([code[s : s + 1] for s in range(4)], 1)
    code_ref[0] = code
    before = jnp.where(
        lax.broadcasted_iota(jnp.int32, (asked, asked), 0) < lax.broadcasted_iota(jnp.int32, (asked, asked), 1), 1.0, 0.0
    ).astype(BF16)
    slot_at = lax.broadcasted_iota(jnp.int32, (8, asked), 0)

    def by_slot(values):
        out = jnp.zeros((8, asked), F32)
        for n, value in enumerate(values):
            out = jnp.where(slot_at == n, float(value), out)
        return out

    def ranks(offset):
        ok = jnp.logical_and(offset >= 0.0, offset < cells)
        return ok, bmm(jnp.where(ok, 1.0, 0.0).astype(BF16), before)

    offset = jnp.broadcast_to(code, (8, asked)) - by_slot([cells * (3 * (dx + 1) + dy + 1) for dx, dy in OFFS])
    ok, rank = ranks(offset)
    late = jnp.where(jnp.logical_and(ok, rank >= by_slot(CAPS)), 1.0, 0.0)
    late = jnp.sum(jnp.sum(late, axis=1, keepdims=True), axis=0, keepdims=True)
    slot = jnp.sum(jnp.where(ok, rank + by_slot(STARTS[:8]), 0.0), axis=0, keepdims=True)
    local = code - 4.0 * cells
    inside = jnp.logical_and(local >= 0.0, local < cells)
    where_at = column(jnp.concatenate([jnp.where(inside, -1.0, slot), jnp.where(inside, local, -1.0)], 0))
    row_ref[0, :, :width] = coarse_ref[...].astype(F32)
    row_ref[0, :, width:] = jnp.broadcast_to(late, (1, 128))
    pl.semaphore_wait(barrier, len(partners))

    asks = [
        send(code_ref, codes_ref.at[pl.ds(BACK[n], 1)], c_send.at[n], c_recv.at[BACK[n]], at(*OFFS[n])) for n in range(8)
    ]
    stage_a = [
        send(row_ref, line_ref.at[pl.ds(j, 1)], a_send.at[k], a_recv.at[k], at(0, k)) for k in range(1, ny)
    ]
    line_ref[pl.ds(j, 1)] = row_ref[...]
    load.wait()
    tile = tile_ref[...].reshape(cells, width)
    lane = lax.broadcasted_iota(jnp.int32, (asked, cells), 1).astype(F32)
    fine = bmm(jnp.where(lane == where_at[:, 1:2], 1.0, 0.0).astype(BF16), tile)
    for ask in asks:
        ask.wait()
    codes = jnp.concatenate([codes_ref[n] for n in range(8)], 0)
    offset = codes - by_slot([cells * (3 * (1 - dx) + 1 - dy) for dx, dy in OFFS])
    ok, rank = ranks(offset)
    rank = jnp.where(ok, rank, -1.0)
    for copy in stage_a:
        copy.wait()
    all_ref[i] = line_ref[...].reshape(ny, width + 128).astype(BF16)
    stage_b = [
        send(all_ref.at[i], all_ref.at[i], b_send.at[k], b_recv.at[k], at(step, 0)) for k, step in enumerate(along_y)
    ]
    moves = []
    for group in ((0, 1, 2, 3), (4, 5, 6, 7)):
        hot = []
        for n in group:
            slots = lax.broadcasted_iota(jnp.int32, (CAPS[n], asked), 0).astype(F32)
            cell = jnp.sum(jnp.where(slots == rank[n : n + 1], offset[n : n + 1], 0.0), axis=1, keepdims=True)
            hot.append(jnp.where(lane[: CAPS[n]] == cell, 1.0, 0.0).astype(BF16))
        low, high = STARTS[group[0]], STARTS[group[-1] + 1]
        out_ref[low:high] = bmm(jnp.concatenate(hot, 0), tile).astype(BF16)
        for n in group:
            src = out_ref.at[pl.ds(STARTS[n], CAPS[n])]
            dst = in_ref.at[pl.ds(STARTS[BACK[n]], CAPS[n])]
            moves.append(send(src, dst, d_send.at[n], d_recv.at[BACK[n]], at(*OFFS[n])))
    for copy in stage_b:
        copy.wait()
    lines = all_ref.at[pl.ds(SIDE * x, SIDE)]
    stage_c = [
        send(lines, lines, b_send.at[SIDE + k], b_recv.at[SIDE + k], at(step, 0)) for k, step in enumerate(along_x)
    ]
    lane = lax.broadcasted_iota(jnp.int32, (asked, STARTS[8]), 1).astype(F32)
    hot = jnp.where(lane == where_at[:, :1], 1.0, 0.0).astype(BF16)
    for copy in moves:
        copy.wait()
    fine_ref[...] = (fine + bmm(hot, in_ref[...])).astype(BF16)
    for copy in stage_c:
        copy.wait()
    full = all_ref[...].astype(F32).reshape(nx * ny, width + 128)
    coarse_out_ref[...] = full[:, :width].astype(BF16)
    flag_ref[...] = jnp.sum(full[:, width:], axis=0, keepdims=True)


def exchange(features, coarse_features, fine_at):
    nx, ny = lax.axis_size("sx"), lax.axis_size("sy")
    rows, cols, width = features.shape
    asked = fine_at.shape[0] * fine_at.shape[1]
    dma = pltpu.SemaphoreType.DMA
    hbm = pl.BlockSpec(memory_space=pltpu.HBM)
    vmem = pl.BlockSpec(memory_space=pltpu.VMEM)
    return pl.pallas_call(
        comm_kernel,
        out_shape=(
            jax.ShapeDtypeStruct((asked, width), BF16),
            jax.ShapeDtypeStruct((nx * ny, width), BF16),
            jax.ShapeDtypeStruct((1, 128), F32),
        ),
        in_specs=[hbm, hbm, hbm],
        out_specs=(vmem, vmem, vmem),
        scratch_shapes=[
            pltpu.VMEM((rows, cols, width), BF16),
            pltpu.VMEM((1, 1, width + 128), F32),
            pltpu.VMEM((ny, 1, width + 128), F32),
            pltpu.VMEM((nx, ny, width + 128), BF16),
            pltpu.VMEM((1, 1, asked), F32),
            pltpu.VMEM((8, 1, asked), F32),
            pltpu.VMEM((STARTS[8], width), BF16),
            pltpu.VMEM((STARTS[8], width), BF16),
            dma((ny,)),
            dma((ny,)),
            dma((2 * SIDE,)),
            dma((2 * SIDE,)),
            dma((8,)),
            dma((8,)),
            dma((8,)),
            dma((8,)),
            dma,
            pltpu.VMEM(coarse_features.shape, BF16),
            pltpu.VMEM(fine_at.shape, jnp.int32),
            dma((2,)),
        ],
        compiler_params=pltpu.CompilerParams(
            collective_id=0, has_side_effects=True, vmem_limit_bytes=32 * 2**20
        ),
    )(features, coarse_features, fine_at)


def padded_2(block, sides, width):
    for axis, dim in sides:
        count = lax.axis_size(axis)
        forward = [(i, (i + 1) % count) for i in range(count)]
        backward = [(target, source) for source, target in forward]
        low = lax.ppermute(
            lax.slice_in_dim(block, block.shape[dim] - width, None, axis=dim), axis, forward
        )
        high = lax.ppermute(lax.slice_in_dim(block, 0, width, axis=dim), axis, backward)
        block = jnp.concatenate([low, block, high], axis=dim)
    return block


def whole_tiles(features, fine_index):
    padded = padded_2(features, (("sx", 0), ("sy", 1)), REACH * SB)
    block_x, block_y = fine_index.shape[:2]
    win = (2 * REACH + 1) * SB
    start_x = (jnp.arange(block_x, dtype=jnp.int32) * SB)[:, None, None]
    start_y = (jnp.arange(block_y, dtype=jnp.int32) * SB)[None, :, None]
    at = (start_x + fine_index // win) * padded.shape[1] + start_y + fine_index % win
    return jnp.take(padded.reshape(-1, padded.shape[2]), at.reshape(-1), axis=0)


def body(features, coarse_features, fine_index, own_order):
    block_x, block_y, fine_count = fine_index.shape
    blocks = block_x * block_y
    fine, coarse, flag = exchange(features, coarse_features, fine_index.reshape(blocks, fine_count))
    fine = lax.cond(flag[0, 0] > 0.0, lambda f: whole_tiles(features, fine_index), lambda f: f, fine)
    vmem = pl.BlockSpec(memory_space=pltpu.VMEM)
    hbm = pl.BlockSpec(memory_space=pltpu.HBM)
    dma = pltpu.SemaphoreType.DMA
    out = pl.pallas_call(
        kernel,
        out_shape=jax.ShapeDtypeStruct((4, 512, 256), F32),
        in_specs=[hbm, vmem, vmem, hbm],
        out_specs=hbm,
        scratch_shapes=[
            pltpu.VMEM((4, 384, 256), BF16),
            pltpu.VMEM((4, 384, 128), F32),
            pltpu.VMEM((4, 128, 384), F32),
            pltpu.VMEM((4, 384, 384), F32),
            pltpu.VMEM((4, 384, 256), F32),
            pltpu.VMEM(features.shape, BF16),
            pltpu.VMEM(own_order.shape, jnp.int32),
            pltpu.VMEM((4, 512, 128), F32),
            pltpu.VMEM((4, 512, 128), F32),
            dma((2,)),
            dma((4,)),
            dma((4,)),
        ],
        compiler_params=pltpu.CompilerParams(vmem_limit_bytes=40 * 2**20),
    )(features, coarse, fine, own_order)
    return out.reshape(block_x, block_y, 512, 256)


def solution(mesh):
    in_specs = (
        P("sx", "sy", None),
        P(("sx", "sy"), None),
        P("sx", "sy", None),
        P("sx", "sy", None),
    )
    out_specs = P("sx", "sy", None, None)
    return jax.shard_map(body, mesh=mesh, in_specs=in_specs, out_specs=out_specs, check_vma=False)
```

```python
import jax
import jax.numpy as jnp
from jax import lax
from jax.experimental import pallas as pl
from jax.experimental.pallas import tpu as pltpu
from jax.sharding import PartitionSpec as P

SB = 16
REACH = 2
NUGGET = 0.3
BS = 32
F32 = jnp.float32
BF16 = jnp.bfloat16
NN = (((1,), (0,)), ((), ()))
NT = (((1,), (1,)), ((), ()))
MESH = pl.DeviceIdType.MESH


def bmm(a, b, dims=NN):
    return lax.dot_general(a, b, dims, preferred_element_type=F32)


def mm(a, b, dims=NN):
    (ca,), (cb,) = dims[0]
    a1, b1 = a.astype(BF16), b.astype(BF16)
    a2, b2 = (a - a1.astype(F32)).astype(BF16), (b - b1.astype(F32)).astype(BF16)
    return bmm(jnp.concatenate([a1, a1, a2], ca), jnp.concatenate([b1, b2, b1], cb), dims)


def lane_pick(x, lane):
    at = (lax.broadcasted_iota(jnp.int32, x.shape, 1) // BS) * BS + lane
    return jnp.take_along_axis(x, at, axis=1)


def sub_pick(x, q):
    return jnp.broadcast_to(x[q : q + 1], (8, 128))


def total(terms):
    while len(terms) > 1:
        terms = [sum(terms[k : k + 2][1:], terms[k]) for k in range(0, len(terms), 2)]
    return terms[0]


def base_block(z):
    vs = [z[8 * v : 8 * v + 8] for v in range(4)]
    li = lax.broadcasted_iota(jnp.int32, (8, 128), 1) % BS
    si = lax.broadcasted_iota(jnp.int32, (8, 128), 0)
    factor = []
    for h in range(2):
        group = (2 * h, 2 * h + 1)
        cols = [[lane_pick(vs[v], 16 * h + q) for v in range(4)] for q in range(16)]
        vs = [
            jnp.where(li // 16 == h, (li == si + 8 * v).astype(F32) if v in group else 0.0, vs[v]) for v in range(4)
        ]
        rows = [jnp.zeros((8, 128), F32)] * 2
        piv = sub_pick(cols[0][2 * h], 0)
        for q in range(16):
            g, sq = group[q // 8], q % 8
            rinv = 1.0 / piv
            plain = sub_pick(vs[g], sq)
            rows[q // 8] = jnp.where(si == sq, plain * lax.rsqrt(piv), rows[q // 8])
            later = {p: sub_pick(cols[p][g], sq) for p in range(q + 1, 16)}
            if q < 15:
                piv = sub_pick(cols[q + 1][group[(q + 1) // 8]], (q + 1) % 8) - later[q + 1] * later[q + 1] * rinv
            for v in group:
                m = cols[q][v]
                m = (jnp.where(si == sq, m - 1.0, m) if v == g else m) * rinv
                vs[v] = vs[v] - m * plain
                for p in later:
                    cols[p][v] = cols[p][v] - m * later[p]
        for v in range(4):
            if v not in group:
                vs[v] = vs[v] - total([cols[q][v] * sub_pick(vs[group[q // 8]], q % 8) for q in range(16)])
        factor += [jnp.where(li <= si + 8 * group[k], rows[k], 0.0) for k in range(2)]
    return jnp.concatenate(vs, 0), jnp.concatenate(factor, 0)


def spread(x, diag):
    return jnp.where(diag, jnp.concatenate([x] * 4, 0), 0.0)


def cut(x, i, u):
    return x[BS * i : BS * i + BS, BS * u : BS * u + BS]


def inner(start, blocks, hook):
    diag = lax.broadcasted_iota(jnp.int32, (128, 128), 0) // BS == lax.broadcasted_iota(jnp.int32, (128, 128), 1) // BS
    zp = [[None] * 4 for _ in range(4)]
    zp[0][0] = jnp.concatenate(start, 1)
    factor = [[] for _ in start]
    for t in range(4):
        if t == 0:
            full = blocks()
            for u in range(4):
                for i in range(4):
                    if u or i:
                        zp[u][i] = jnp.concatenate([cut(b, i, u) for b in full], 1)
        hook(t)
        dinv, w = base_block(zp[t][t])
        src = [spread(zp[u][t], diag) if u != t else None for u in range(4)]
        if t < 3:
            g = mm(jnp.concatenate(zp[t][t + 1 :], 0), spread(dinv, diag))
            for u in sorted(range(4), key=lambda u: u != t + 1):
                change = g if u == t else mm(g, src[u])
                for i in range(t + 1, 4):
                    x = change[BS * (i - t - 1) : BS * (i - t)]
                    zp[u][i] = -x if u == t else zp[u][i] - x
        row = [mm(w, src[u]) for u in range(t)] + [w]
        for s in range(4):
            parts = [x[:, BS * s : BS * s + BS] for x in row]
            parts += [jnp.zeros((BS, BS * (3 - t)), F32)] if t < 3 else []
            factor[s].append(jnp.concatenate(parts, 1))
    return [jnp.concatenate(f, 0) for f in factor]


def squares(x):
    xf = x.astype(F32)
    x2 = xf * xf
    hi = x2.astype(BF16)
    lo = (x2 - hi.astype(F32)).astype(BF16)
    ones = jnp.ones((8, x.shape[1]), BF16)
    row = (bmm(ones, hi, NT) + bmm(ones, lo, NT))[:1]
    return jnp.sum(x2, axis=1, keepdims=True), row


def theta(a, b, sa, sb, shift=None):
    t = jnp.exp((2.0 * bmm(a, b, NT) - (sa + sb)) * (1.0 / a.shape[1]))
    if shift is not None:
        i, j = lax.broadcasted_iota(jnp.int32, t.shape, 0), lax.broadcasted_iota(jnp.int32, t.shape, 1)
        t = jnp.where(i + shift == j, 1.0 + NUGGET, t)
    return t


def column(x):
    x = x.astype(F32)
    pad = jnp.zeros((8 - x.shape[0], x.shape[1]), F32)
    return jnp.concatenate([x, pad], 0).T


def kernel(
    feat_hbm, coarse_ref, fine_ref, own_hbm, out_hbm,
    p_ref, k_ref, kt_ref, th_ref, e_ref, feat_ref, own_ref, lo_ref, hi_ref, in_sem, lo_sem, hi_sem,
):
    loads = [
        pltpu.make_async_copy(own_hbm, own_ref, in_sem.at[0]),
        pltpu.make_async_copy(feat_hbm, feat_ref, in_sem.at[1]),
    ]
    for load in loads:
        load.start()
    width = feat_ref.shape[2]
    n = 128
    four = range(4)
    pc = coarse_ref[...]
    sc_col, sc_row = squares(pc)
    acc = theta(pc, pc, sc_col, sc_row, 0)
    for load in loads:
        load.wait()
    own_at = column(jnp.concatenate([own_ref[0], own_ref[1]], 0))
    lane = lax.broadcasted_iota(jnp.int32, (256, 256), 1).astype(F32)

    def kernel_matrix(s):
        bx, by = divmod(s, 2)
        own = feat_ref[SB * bx : SB * bx + SB, SB * by : SB * by + SB].reshape(256, width)
        hot = jnp.where(lane == own_at[:, s : s + 1], 1.0, 0.0).astype(BF16)
        p_ref[s, n:] = bmm(hot, own).astype(BF16)
        p_ref[s, :n] = fine_ref[n * s : n * s + n]
        p = p_ref[s]
        col, row = squares(p)
        k_ref[s] = theta(p, pc, col, sc_row)
        kt_ref[s] = theta(pc, p, sc_col, row)
        th_ref[s, :, :n] = theta(p, p[:n], col, row[:, :n], 0)
        th_ref[s, n : 2 * n, n : 2 * n] = theta(p[n : 2 * n], p[n : 2 * n], col[n : 2 * n], row[:, n : 2 * n], 0)
        th_ref[s, 2 * n :, n:] = theta(p[2 * n :], p[n:], col[2 * n :], row[:, n:], n)

    wc = inner([cut(acc, 0, 0)] * 4, lambda: [acc] * 4, kernel_matrix)[0]

    def leading(rows, s, at):
        own = rows[BS * s : BS * s + BS]
        return th_ref[s, at : at + BS, at : at + BS] - mm(own, own, NT)

    kf = []

    def fine_block():
        x = mm(jnp.concatenate([k_ref[s, :n] for s in four], 0), wc, NT)
        kf.extend(x[n * s : n * s + n] for s in four)
        return [th_ref[s, :n, :n] - mm(kf[s], kf[s], NT) for s in four]

    def leave_coarse(s):
        ko = mm(k_ref[s, n:], wc, NT)
        th_ref[s, n:, :n] = th_ref[s, n:, :n] - mm(ko, kf[s], NT)
        th_ref[s, n : 2 * n, n : 2 * n] = th_ref[s, n : 2 * n, n : 2 * n] - mm(ko[:n], ko[:n], NT)
        th_ref[s, 2 * n :, n:] = th_ref[s, 2 * n :, n:] - mm(ko[n:], ko, NT)

    head = mm(jnp.concatenate([k_ref[s, :BS] for s in four], 0), wc, NT)
    wf = inner([leading(head, s, 0) for s in four], fine_block, leave_coarse)

    lof = []
    cinv = mm(wc.T, wc)

    def own_block():
        lof.extend(mm(th_ref[s, n : 2 * n, :n], wf[s], NT) for s in four)
        return [th_ref[s, n : 2 * n, n : 2 * n] - mm(lof[s], lof[s], NT) for s in four]

    def leave_fine(s):
        low = mm(th_ref[s, 2 * n :, :n], wf[s], NT)
        both = jnp.concatenate([lof[s], low], 0)
        th_ref[s, 2 * n :, n:] = th_ref[s, 2 * n :, n:] - mm(low, both, NT)
        qt = mm(both, wf[s]).T
        ht = mm(cinv, kt_ref[s])
        e_ref[s, :n] = mm(ht[:, :n], qt) - ht[:, n:]
        e_ref[s, n : 2 * n] = -qt

    head = jnp.concatenate([mm(th_ref[s, n : n + BS, :n], wf[s], NT) for s in four], 0)
    w0 = inner([leading(head, s, n) for s in four], own_block, leave_fine)

    l10 = []
    stores = []

    def last_block():
        l10.extend(mm(th_ref[s, 2 * n :, n : 2 * n], w0[s], NT) for s in four)
        return [th_ref[s, 2 * n :, 2 * n :] - mm(l10[s], l10[s], NT) for s in four]

    def first_half(s):
        top = mm(e_ref[s, : 2 * n, :n], w0[s], NT)
        w0t = w0[s].T
        lo_ref[s, : 2 * n] = top
        lo_ref[s, 2 * n : 3 * n] = w0t
        lo_ref[s, 3 * n :] = jnp.zeros((n, n), F32)
        stores.append(pltpu.make_async_copy(lo_ref.at[s], out_hbm.at[s, :, pl.ds(0, n)], lo_sem.at[s]))
        stores[-1].start()
        e_ref[s, : 2 * n, n:] = e_ref[s, : 2 * n, n:] - mm(top, l10[s], NT)
        e_ref[s, 2 * n :, n:] = -mm(w0t, l10[s], NT)

    head = jnp.concatenate([mm(th_ref[s, 2 * n : 2 * n + BS, n : 2 * n], w0[s], NT) for s in four], 0)
    w1 = inner([leading(head, s, 2 * n) for s in four], last_block, first_half)
    for s in four:
        hi_ref[s, : 3 * n] = mm(e_ref[s, :, n:], w1[s], NT)
        hi_ref[s, 3 * n :] = w1[s].T
        stores.append(pltpu.make_async_copy(hi_ref.at[s], out_hbm.at[s, :, pl.ds(n, n)], hi_sem.at[s]))
        stores[-1].start()
    for store in stores:
        store.wait()


OFFS = ((-1, -1), (-1, 1), (1, -1), (1, 1), (-1, 0), (0, -1), (0, 1), (1, 0))
BACK = (3, 2, 1, 0, 7, 6, 5, 4)
SIDE = 4
CAPS = tuple(112 if 0 in o else 80 for o in OFFS)
STARTS = tuple(sum(CAPS[:n]) for n in range(9))


def comm_kernel(
    feat_ref, coarse_hbm, fine_at_hbm, fine_ref, coarse_out_ref, flag_ref,
    tile_ref, row_ref, line_ref, all_ref, code_ref, codes_ref, out_ref, in_ref,
    a_send, a_recv, b_send, b_recv, c_send, c_recv, d_send, d_recv, tile_sem, coarse_ref, fine_at_ref, in_sem,
):
    nx, ny = lax.axis_size("sx"), lax.axis_size("sy")
    i, j = lax.axis_index("sx"), lax.axis_index("sy")
    rows, cols, width = feat_ref.shape
    cells = rows * cols
    asked = fine_at_ref.shape[0] * fine_at_ref.shape[1]

    def at(dx, dy):
        return {"sx": lax.rem(i + dx + nx, nx), "sy": lax.rem(j + dy + ny, ny)}

    def send(src, dst, s_sem, r_sem, device):
        copy = pltpu.make_async_remote_copy(
            src_ref=src, dst_ref=dst, send_sem=s_sem, recv_sem=r_sem, device_id=device, device_id_type=MESH
        )
        copy.start()
        return copy

    small = [
        pltpu.make_async_copy(fine_at_hbm, fine_at_ref, in_sem.at[0]),
        pltpu.make_async_copy(coarse_hbm, coarse_ref, in_sem.at[1]),
    ]
    for copy in small:
        copy.start()
    load = pltpu.make_async_copy(feat_ref, tile_ref, tile_sem)
    load.start()
    barrier = pltpu.get_barrier_semaphore()
    x, y = i // SIDE, lax.rem(i, SIDE)
    along_y = [lax.rem(y + k, SIDE) - y for k in range(1, SIDE)]
    along_x = [SIDE * k for k in range(1, nx // SIDE)]
    partners = [(dx, dy) for dx, dy in OFFS if dx]
    partners += [(0, k) for k in range(1, ny)] + [(k, 0) for k in along_y] + [(k, 0) for k in along_x]
    for dx, dy in partners:
        pl.semaphore_signal(barrier, inc=1, device_id=at(dx, dy), device_id_type=MESH)

    for copy in small:
        copy.wait()
    f = fine_at_ref[...]
    win_row = lax.shift_right_logical(f * 52429, 22)
    s_at = lax.broadcasted_iota(jnp.int32, f.shape, 0)
    r = win_row + SB * lax.shift_right_logical(s_at, 1)
    c = f - 80 * win_row + SB * lax.bitwise_and(s_at, 1)
    t9 = 3 * lax.shift_right_logical(r, 5) + lax.shift_right_logical(c, 5)
    code = cells * t9 + 32 * lax.bitwise_and(r, 31) + lax.bitwise_and(c, 31)
    code = code.astype(F32)
    code = jnp.concatenate([code[s : s + 1] for s in range(4)], 1)
    code_ref[0] = code
    before = jnp.where(
        lax.broadcasted_iota(jnp.int32, (asked, asked), 0) < lax.broadcasted_iota(jnp.int32, (asked, asked), 1), 1.0, 0.0
    ).astype(BF16)
    slot_at = lax.broadcasted_iota(jnp.int32, (8, asked), 0)

    def by_slot(values):
        out = jnp.zeros((8, asked), F32)
        for n, value in enumerate(values):
            out = jnp.where(slot_at == n, float(value), out)
        return out

    def ranks(offset):
        ok = jnp.logical_and(offset >= 0.0, offset < cells)
        return ok, bmm(jnp.where(ok, 1.0, 0.0).astype(BF16), before)

    offset = jnp.broadcast_to(code, (8, asked)) - by_slot([cells * (3 * (dx + 1) + dy + 1) for dx, dy in OFFS])
    ok, rank = ranks(offset)
    late = jnp.where(jnp.logical_and(ok, rank >= by_slot(CAPS)), 1.0, 0.0)
    late = jnp.sum(jnp.sum(late, axis=1, keepdims=True), axis=0, keepdims=True)
    slot = jnp.sum(jnp.where(ok, rank + by_slot(STARTS[:8]), 0.0), axis=0, keepdims=True)
    local = code - 4.0 * cells
    inside = jnp.logical_and(local >= 0.0, local < cells)
    where_at = column(jnp.concatenate([jnp.where(inside, -1.0, slot), jnp.where(inside, local, -1.0)], 0))
    row_ref[0, :, :width] = coarse_ref[...].astype(F32)
    row_ref[0, :, width:] = jnp.broadcast_to(late, (1, 128))
    pl.semaphore_wait(barrier, len(partners))

    asks = [
        send(code_ref, codes_ref.at[pl.ds(BACK[n], 1)], c_send.at[n], c_recv.at[BACK[n]], at(*OFFS[n])) for n in range(8)
    ]
    stage_a = [
        send(row_ref, line_ref.at[pl.ds(j, 1)], a_send.at[k], a_recv.at[k], at(0, k)) for k in range(1, ny)
    ]
    line_ref[pl.ds(j, 1)] = row_ref[...]
    load.wait()
    tile = tile_ref[...].reshape(cells, width)
    lane = lax.broadcasted_iota(jnp.int32, (asked, cells), 1).astype(F32)
    fine = bmm(jnp.where(lane == where_at[:, 1:2], 1.0, 0.0).astype(BF16), tile)
    for ask in asks:
        ask.wait()
    codes = jnp.concatenate([codes_ref[n] for n in range(8)], 0)
    offset = codes - by_slot([cells * (3 * (1 - dx) + 1 - dy) for dx, dy in OFFS])
    ok, rank = ranks(offset)
    rank = jnp.where(ok, rank, -1.0)
    for copy in stage_a:
        copy.wait()
    all_ref[i] = line_ref[...].reshape(ny, width + 128).astype(BF16)
    stage_b = [
        send(all_ref.at[i], all_ref.at[i], b_send.at[k], b_recv.at[k], at(step, 0)) for k, step in enumerate(along_y)
    ]
    moves = []
    for group in ((0, 1, 2, 3), (4, 5, 6, 7)):
        hot = []
        for n in group:
            slots = lax.broadcasted_iota(jnp.int32, (CAPS[n], asked), 0).astype(F32)
            cell = jnp.sum(jnp.where(slots == rank[n : n + 1], offset[n : n + 1], 0.0), axis=1, keepdims=True)
            hot.append(jnp.where(lane[: CAPS[n]] == cell, 1.0, 0.0).astype(BF16))
        low, high = STARTS[group[0]], STARTS[group[-1] + 1]
        out_ref[low:high] = bmm(jnp.concatenate(hot, 0), tile).astype(BF16)
        for n in group:
            src = out_ref.at[pl.ds(STARTS[n], CAPS[n])]
            dst = in_ref.at[pl.ds(STARTS[BACK[n]], CAPS[n])]
            moves.append(send(src, dst, d_send.at[n], d_recv.at[BACK[n]], at(*OFFS[n])))
    for copy in stage_b:
        copy.wait()
    lines = all_ref.at[pl.ds(SIDE * x, SIDE)]
    stage_c = [
        send(lines, lines, b_send.at[SIDE + k], b_recv.at[SIDE + k], at(step, 0)) for k, step in enumerate(along_x)
    ]
    lane = lax.broadcasted_iota(jnp.int32, (asked, STARTS[8]), 1).astype(F32)
    hot = jnp.where(lane == where_at[:, :1], 1.0, 0.0).astype(BF16)
    for copy in moves:
        copy.wait()
    fine_ref[...] = (fine + bmm(hot, in_ref[...])).astype(BF16)
    for copy in stage_c:
        copy.wait()
    full = all_ref[...].astype(F32).reshape(nx * ny, width + 128)
    coarse_out_ref[...] = full[:, :width].astype(BF16)
    flag_ref[...] = jnp.sum(full[:, width:], axis=0, keepdims=True)


def exchange(features, coarse_features, fine_at):
    nx, ny = lax.axis_size("sx"), lax.axis_size("sy")
    rows, cols, width = features.shape
    asked = fine_at.shape[0] * fine_at.shape[1]
    dma = pltpu.SemaphoreType.DMA
    hbm = pl.BlockSpec(memory_space=pltpu.HBM)
    vmem = pl.BlockSpec(memory_space=pltpu.VMEM)
    return pl.pallas_call(
        comm_kernel,
        out_shape=(
            jax.ShapeDtypeStruct((asked, width), BF16),
            jax.ShapeDtypeStruct((nx * ny, width), BF16),
            jax.ShapeDtypeStruct((1, 128), F32),
        ),
        in_specs=[hbm, hbm, hbm],
        out_specs=(vmem, vmem, vmem),
        scratch_shapes=[
            pltpu.VMEM((rows, cols, width), BF16),
            pltpu.VMEM((1, 1, width + 128), F32),
            pltpu.VMEM((ny, 1, width + 128), F32),
            pltpu.VMEM((nx, ny, width + 128), BF16),
            pltpu.VMEM((1, 1, asked), F32),
            pltpu.VMEM((8, 1, asked), F32),
            pltpu.VMEM((STARTS[8], width), BF16),
            pltpu.VMEM((STARTS[8], width), BF16),
            dma((ny,)),
            dma((ny,)),
            dma((2 * SIDE,)),
            dma((2 * SIDE,)),
            dma((8,)),
            dma((8,)),
            dma((8,)),
            dma((8,)),
            dma,
            pltpu.VMEM(coarse_features.shape, BF16),
            pltpu.VMEM(fine_at.shape, jnp.int32),
            dma((2,)),
        ],
        compiler_params=pltpu.CompilerParams(
            collective_id=0, has_side_effects=True, vmem_limit_bytes=32 * 2**20
        ),
    )(features, coarse_features, fine_at)


def padded_2(block, sides, width):
    for axis, dim in sides:
        count = lax.axis_size(axis)
        forward = [(i, (i + 1) % count) for i in range(count)]
        backward = [(target, source) for source, target in forward]
        low = lax.ppermute(
            lax.slice_in_dim(block, block.shape[dim] - width, None, axis=dim), axis, forward
        )
        high = lax.ppermute(lax.slice_in_dim(block, 0, width, axis=dim), axis, backward)
        block = jnp.concatenate([low, block, high], axis=dim)
    return block


def whole_tiles(features, fine_index):
    padded = padded_2(features, (("sx", 0), ("sy", 1)), REACH * SB)
    block_x, block_y = fine_index.shape[:2]
    win = (2 * REACH + 1) * SB
    start_x = (jnp.arange(block_x, dtype=jnp.int32) * SB)[:, None, None]
    start_y = (jnp.arange(block_y, dtype=jnp.int32) * SB)[None, :, None]
    at = (start_x + fine_index // win) * padded.shape[1] + start_y + fine_index % win
    return jnp.take(padded.reshape(-1, padded.shape[2]), at.reshape(-1), axis=0)


def body(features, coarse_features, fine_index, own_order):
    block_x, block_y, fine_count = fine_index.shape
    blocks = block_x * block_y
    fine, coarse, flag = exchange(features, coarse_features, fine_index.reshape(blocks, fine_count))
    fine = lax.cond(flag[0, 0] > 0.0, lambda f: whole_tiles(features, fine_index), lambda f: f, fine)
    vmem = pl.BlockSpec(memory_space=pltpu.VMEM)
    hbm = pl.BlockSpec(memory_space=pltpu.HBM)
    dma = pltpu.SemaphoreType.DMA
    out = pl.pallas_call(
        kernel,
        out_shape=jax.ShapeDtypeStruct((4, 512, 256), F32),
        in_specs=[hbm, vmem, vmem, hbm],
        out_specs=hbm,
        scratch_shapes=[
            pltpu.VMEM((4, 384, 256), BF16),
            pltpu.VMEM((4, 384, 128), F32),
            pltpu.VMEM((4, 128, 384), F32),
            pltpu.VMEM((4, 384, 384), F32),
            pltpu.VMEM((4, 384, 256), F32),
            pltpu.VMEM(features.shape, BF16),
            pltpu.VMEM(own_order.shape, jnp.int32),
            pltpu.VMEM((4, 512, 128), F32),
            pltpu.VMEM((4, 512, 128), F32),
            dma((2,)),
            dma((4,)),
            dma((4,)),
        ],
        compiler_params=pltpu.CompilerParams(vmem_limit_bytes=40 * 2**20),
    )(features, coarse, fine, own_order)
    return out.reshape(block_x, block_y, 512, 256)


def solution(mesh):
    in_specs = (
        P("sx", "sy", None),
        P(("sx", "sy"), None),
        P("sx", "sy", None),
        P("sx", "sy", None),
    )
    out_specs = P("sx", "sy", None, None)
    return jax.shard_map(body, mesh=mesh, in_specs=in_specs, out_specs=out_specs, check_vma=False)
```
